32 devices in a mesh: node: 4 (over z), band: 8 (over y, x, core).
Axes of the slice: x: 2, y: 2, z: 4, core: 2. Of those that a mesh axis runs over, the one named last changes fastest.
Arguments:
- state0: float32 [2, 1024, 4, 3, 512], P(None, 'band'), may hold values from -36 to 36
- iterate: float32 [4, 2, 1024, 4, 3, 512], P('node', None, 'band'), may hold values from -37.2 to 37.2
- legendre: bfloat16 [1024, 512, 512], P('band'), may hold values from -0.25 to 0.25
- lat_weight: float32 [512], replicated, may hold values from 0.25 to 1
- coriolis: float32 [2, 512], replicated, may hold values from -1.5 to 1.5
- damping: float32 [1024, 3, 512], P('band'), may hold values from 0.1 to 10
- quadrature: float32 [4, 4], replicated, may hold values from 0.02 to 0.25
Outputs:
- updated: float32 [4, 2, 1024, 4, 3, 512], P('node', None, 'band')
- sweep_change: float32 [3], replicated
The draws below stay inside these ranges and needn't reach their ends.
All inputs are finite; a program needn't handle non-finite values.
Results may differ from the reference program's by a relative error of at most 0.0017.
Values may be sent and summed in bfloat16 or wider, within the bound.
A program may use at most 256 MiB of HBM per device.

```python
import math
import jax
import jax.numpy as jnp
from jax import lax

M = 1024
J = 512
NH = 512
ENS = 4
NLON = 2048
NODES = 4


def base_field(key):
    noise_key, row_key, col_key = jax.random.split(key, 3)
    shape = (2, M, ENS, 3, J)
    noise = jnp.clip(jax.random.normal(noise_key, shape, jnp.float32), -4.0, 4.0)
    low = math.log(0.3)
    high = math.log(3.0)
    rows = jnp.exp(jax.random.uniform(row_key, (1, M, 1, 3, 1), jnp.float32, low, high))
    cols = jnp.exp(jax.random.uniform(col_key, (1, 1, 1, 1, J), jnp.float32, low, high))
    return noise * rows * cols


def draw_state0(key, part):
    return base_field(jax.random.fold_in(key, 11)).astype(jnp.float32)


def draw_iterate(key, part):
    start = base_field(jax.random.fold_in(key, 11))
    noise = jnp.clip(jax.random.normal(jax.random.fold_in(key, 12), (NODES,) + start.shape, jnp.float32), -4.0, 4.0)
    return (start[None] + 0.3 * noise).astype(jnp.float32)


def levels(key, extent, cuts, smallest, high):
    loudness = 1.0
    for position, blocks in cuts:
        heights = jax.random.uniform(jax.random.fold_in(jax.random.fold_in(key, 6), position), (blocks,), jnp.float32, smallest / len(cuts), high / len(cuts))
        loudness = loudness * jnp.repeat(jnp.exp(heights), extent[position] // blocks).reshape((-1,) + (1,) * (len(extent) - 1 - position))
    return loudness


def gaussian(key, extent, spread, limit, cuts=(), kind=jnp.bfloat16):
    gain = levels(key, extent, cuts, -0.22, 0.18) if cuts else 1.0
    drawn = jax.random.normal(key, extent, jnp.float32) * spread * gain
    return jnp.minimum(jnp.maximum(drawn, -limit), limit).astype(kind)


def setup_inputs(seed: int = 0) -> dict:
    keys = jax.random.split(jax.random.key(seed), 8)
    return {
        "state0": draw_state0(jax.random.fold_in(keys[7], 71), 0),
        "iterate": draw_iterate(jax.random.fold_in(keys[7], 71), 0),
        "legendre": gaussian(keys[2], (M, NH, J), J ** -0.5, 0.25, ((0, 8),)),
        "lat_weight": jnp.clip(jax.random.uniform(keys[3], (NH,), jnp.float32, 0.25, 1.0), 0.25, 1.0),
        "coriolis": jnp.clip(jax.random.uniform(keys[4], (2, NH), jnp.float32, -1.5, 1.5), -1.5, 1.5),
        "damping": jnp.clip(jnp.exp(math.log(10.0) - 4.6051702 * jax.random.uniform(keys[5], (M, 3, J), jnp.float32) ** levels(keys[5], (M, 3, J), ((0, 8),), -0.2, 0.2)), 0.1, 10.0),
        "quadrature": jnp.clip(jax.random.uniform(keys[6], (NODES, NODES), jnp.float32, 0.02, 0.25), 0.02, 0.25),
    }


def to_grid(coeffs):
    first = (2.0 * jnp.real(coeffs[..., :1])).astype(coeffs.dtype)
    tail = jnp.zeros(coeffs.shape[:-1] + (NLON // 2 + 1 - M,), coeffs.dtype)
    padded = jnp.concatenate([first, coeffs[..., 1:], tail], axis=-1)
    return math.sqrt(M) * jnp.fft.irfft(padded, n=NLON, axis=-1)

def node_force(spec, legendre, lat_weight, coriolis, damping):
    half = J // 2
    table = legendre.astype(jnp.float32)
    coeff = spec.astype(jnp.bfloat16).astype(jnp.float32)
    even = jnp.einsum('cmefj,mlj->cmefl', coeff[..., :half], table[:, :, :half])
    odd = jnp.einsum('cmefj,mlj->cmefl', coeff[..., half:], table[:, :, half:])
    four = jnp.stack([even + odd, even - odd], axis=4)
    four = jnp.transpose(four, (0, 2, 3, 4, 5, 1))
    comp = four[0] + 1j * four[1]
    wave = jnp.arange(M, dtype=jnp.float32) / M
    values = to_grid(comp)
    slopes = to_grid(1j * wave * comp)
    u_wind, v_wind, height = (values[:, 0], values[:, 1], values[:, 2])
    u_slope, v_slope, h_slope = (slopes[:, 0], slopes[:, 1], slopes[:, 2])
    cor = coriolis[:, :, None]
    tend_u = -u_wind * u_slope + cor * v_wind - h_slope
    tend_v = -u_wind * v_slope - cor * u_wind
    tend_h = -u_wind * h_slope - (1.0 + height) * u_slope
    tend = jnp.stack([tend_u, tend_v, tend_h], axis=1)
    spectrum = jnp.fft.rfft(tend, axis=-1)[..., :M] / math.sqrt(M)
    weight = lat_weight[:, None]
    sym = weight * (spectrum[:, :, 0] + spectrum[:, :, 1])
    anti = weight * (spectrum[:, :, 0] - spectrum[:, :, 1])

    def to_real(z):
        parts = jnp.stack([jnp.real(z), jnp.imag(z)], axis=0)
        parts = jnp.transpose(parts, (0, 4, 1, 2, 3))
        return parts.astype(jnp.bfloat16).astype(jnp.float32)
    sym_r = to_real(sym)
    anti_r = to_real(anti)
    spec_even = jnp.einsum('cmefl,mlj->cmefj', sym_r, table[:, :, :half])
    spec_odd = jnp.einsum('cmefl,mlj->cmefj', anti_r, table[:, :, half:])
    nonlinear = jnp.concatenate([spec_even, spec_odd], axis=-1)
    return nonlinear - damping[None, :, None] * spec

def reference(state0, iterate, legendre, lat_weight, coriolis, damping, quadrature):
    force = lax.map(lambda spec: node_force(spec, legendre, lat_weight, coriolis, damping), iterate)
    mixed = jnp.tensordot(quadrature, force, axes=1, precision=lax.Precision.HIGHEST)
    diag = jnp.diagonal(quadrature)[:, None, None, None, None, None]
    rate = damping[None, None, :, None, :, :]
    updated = (state0[None] + mixed + diag * rate * iterate) / (1.0 + diag * rate)
    change = lax.optimization_barrier(jnp.sum((updated - iterate) ** 2, axis=(0, 1, 2, 3, 5)))
    base = lax.optimization_barrier(jnp.sum(state0 ** 2, axis=(0, 1, 2, 4)))
    sweep_change = jnp.sqrt(change / (NODES * base + 1e-06))
    return (updated, sweep_change)
```

```python
import functools
import math

import jax
import jax.numpy as jnp
import numpy as np
from jax import lax
from jax.experimental import pallas as pl
from jax.experimental.pallas import tpu as pltpu
from jax.sharding import PartitionSpec as P

MESH = pl.DeviceIdType.MESH
F32, BF16 = jnp.float32, jnp.bfloat16
VMEM_BYTES = 63_000_000
LANES = 128
SUB = 4


def split_bf16(x):
    high = lax.reduce_precision(x, 8, 7)
    return high.astype(jnp.bfloat16), (x - high).astype(jnp.bfloat16)


def dft_table(parity, nband, local_modes, modes, points):
    fine = 32
    coarse = modes // fine
    column = lax.iota(jnp.int32, modes)
    pairs = local_modes // 2
    part = column // pairs % 2
    wave = column // local_modes * local_modes + column % pairs * 2 + parity
    unit = 2.0 * math.pi / points

    def angle(index):
        return (index % points).astype(jnp.float32) * unit

    big = angle(
        lax.iota(jnp.int32, coarse)[:, None] * fine * wave[None] + part[None] * (points // 4)
    )
    small = angle(lax.iota(jnp.int32, fine)[:, None] * wave[None])
    cos_big, sin_big = jnp.cos(big)[:, None], jnp.sin(big)[:, None]
    cos_small, sin_small = jnp.cos(small)[None], jnp.sin(small)[None]
    scale = 1.0 / math.sqrt(modes)
    slope_scale = wave.astype(jnp.float32) * (scale / modes)
    value = (cos_big * cos_small - sin_big * sin_small).reshape(modes, modes) * scale
    slope = -(sin_big * cos_small + cos_big * sin_small).reshape(modes, modes) * slope_scale
    return split_bf16(value), split_bf16(slope)


def mul(a, b, dims):
    return lax.dot_general(a, b, (dims, ((), ())), preferred_element_type=jnp.float32)


def plain_body(state0, iterate, legendre, lat_weight, coriolis, damping, quadrature):
    spec = iterate[0]
    degrees = legendre.shape[2]
    half = degrees // 2
    local_modes, hemi = legendre.shape[:2]
    members, fields = spec.shape[2:4]
    nband = lax.axis_size("band")
    nnode = lax.axis_size("node")
    modes = local_modes * nband
    points = 2 * modes
    pairs = local_modes // 2
    lat_rows = hemi // nband
    node = lax.axis_index("node")
    band = lax.axis_index("band")
    tables = [dft_table(p, nband, local_modes, modes, points) for p in range(2)]
    cor = lax.dynamic_slice_in_dim(coriolis, band * lat_rows, lat_rows, 1)
    weight = lax.dynamic_slice_in_dim(lat_weight, band * lat_rows, lat_rows, 0)
    quad_row = lax.dynamic_slice_in_dim(quadrature, node, 1, 0)[0]
    diag = lax.dynamic_slice(quadrature, (node, node), (1, 1))[0, 0]
    is_even = lax.iota(jnp.int32, degrees) < half
    rate = damping[None, :, None]

    groups = 2
    ens = members // groups

    def synthesis(first):
        coeff = spec[:, :, first : first + ens].astype(jnp.bfloat16)
        coeff = coeff.transpose(1, 0, 3, 2, 4)
        zero = jnp.zeros((), jnp.bfloat16)
        rows = jnp.stack([jnp.where(is_even, coeff, zero), jnp.where(is_even, zero, coeff)], axis=1)
        rows = rows.reshape(local_modes, 4 * fields * ens, degrees)
        four = jnp.einsum("mrj,mlj->mrl", rows, legendre, preferred_element_type=jnp.float32)
        four = four.astype(jnp.bfloat16)
        four = four.reshape(pairs, 2, 2, 2, fields, ens, nband, lat_rows)
        four = four.transpose(6, 1, 3, 0, 2, 4, 5, 7)
        four = four.reshape(nband, 2, 2, pairs, 2 * fields * ens * lat_rows)
        return lax.all_to_all(four, "band", split_axis=0, concat_axis=0, tiled=True)

    def grid_step(four):
        shape = (modes, 2, fields, ens * lat_rows)
        parts = []
        for p in range(2):
            x = four[:, p].reshape(modes, -1)
            pair = []
            for high, low in tables[p]:
                dims = ((1,), (0,))
                pair.append((mul(high, x, dims) + mul(low, x, dims)).reshape(shape))
            parts.append(pair)
        tends = []
        for h in range(2):
            value, slope = (
                parts[0][v] + parts[1][v] if h == 0 else parts[0][v] - parts[1][v] for v in range(2)
            )
            hemis = []
            for s in range(2):
                val, slo = (
                    g[:, 0] + g[:, 1] if s == 0 else g[:, 0] - g[:, 1] for g in (value, slope)
                )
                c = jnp.tile(cor[s], ens)
                u, v, z = (val[:, f] for f in range(3))
                du, dv, dz = (slo[:, f] for f in range(3))
                hemis.append(
                    jnp.stack(
                        [-u * du + c * v - dz, -u * dv - c * u, -u * dz - (1.0 + z) * du], axis=1
                    )
                )
            tends.append(jnp.stack([hemis[0] + hemis[1], hemis[0] - hemis[1]], axis=1))
        scale = jnp.tile(weight, 2 * fields * ens)
        spectra = []
        for p in range(2):
            z = tends[0] + tends[1] if p == 0 else tends[0] - tends[1]
            zh, zl = split_bf16(z.reshape(modes, -1))
            high, low = tables[p][0]
            dims = ((0,), (0,))
            s = mul(high, zh, dims) + mul(high, zl, dims) + mul(low, zh, dims)
            spectra.append((s * scale).astype(jnp.bfloat16).reshape(nband, 2, pairs, -1))
        out = jnp.stack(spectra, axis=1)
        return lax.all_to_all(out, "band", split_axis=0, concat_axis=0, tiled=True)

    def analysis(out, first):
        out = out.reshape(nband, 2, 2, pairs, 2, fields, ens, lat_rows)
        out = out.transpose(3, 1, 4, 2, 5, 6, 0, 7)
        out = out.reshape(local_modes, 4 * fields * ens, hemi)
        both = jnp.einsum("mrl,mlj->mrj", out, legendre, preferred_element_type=jnp.float32)
        both = both.reshape(local_modes, 2, 2, fields, ens, degrees)
        nonlinear = jnp.where(is_even, both[:, 0], both[:, 1]).transpose(1, 0, 3, 2, 4)
        part = slice(first, first + ens)
        rest = nonlinear - rate * (spec[:, :, part] - state0[:, :, part])
        gathered = lax.all_gather(rest.astype(jnp.bfloat16), "node")
        mixed = sum(quad_row[p] * gathered[p].astype(jnp.float32) for p in range(nnode))
        return mixed

    received = [synthesis(g * ens) for g in range(groups)]
    spectra = [grid_step(r) for r in received]
    mixed = [analysis(s, g * ens) for g, s in enumerate(spectra)]
    mixed = jnp.concatenate(mixed, axis=2) - jnp.sum(quad_row) * (rate * state0)
    updated = (state0 + mixed + diag * rate * spec) / (1.0 + diag * rate)
    change = jnp.sum((updated - spec) ** 2, axis=(0, 1, 2, 4))
    base = jnp.sum(state0 * state0, axis=(0, 1, 2, 4))
    total = lax.psum(jnp.stack([change, base]), ("node", "band"))
    ratio = jnp.sqrt(total[0] / (total[1] + 1e-06))
    return (updated[None], ratio)


class Plan:
    def __init__(self, nband, nnode, iterate, legendre):
        self.n, self.nnode = nband, nnode
        self.modes, self.members, self.fields, self.degrees = iterate[2:]
        self.hemi = legendre[1]
        self.ml = self.modes // nband
        self.lb = LANES
        self.nlb = self.hemi // self.lb
        self.eg = max(nband // max(self.nlb, 1), 1)
        self.el = self.members // self.eg
        self.rows = 2 * self.members * self.fields
        self.pl = self.ml // 2
        self.mc = 32
        self.nc = self.ml // self.mc
        self.half = self.modes // 2
        self.kc = (self.half + 16) // 3
        self.g = 4 * self.fields
        self.fits = (
            nnode == 4
            and self.fields == 3
            and self.nlb * self.eg == nband
            and self.eg * self.el == self.members
            and self.hemi % self.lb == 0
            and self.ml % self.mc == 0
            and self.modes % nband == 0
            and (self.half + 16) % 48 == 0
            and self.rows % 8 == 0
            and self.degrees % 256 == 0
        )


def greet(axis, peers):
    sem = pltpu.get_barrier_semaphore()
    for peer in peers:
        pl.semaphore_signal(sem, inc=1, device_id={axis: peer}, device_id_type=MESH)
    pl.semaphore_wait(sem, len(peers))


def gather_rows(d, rows, piece):
    for cc in range(2):
        for e in range(d.members):
            r = (cc * d.members + e) * d.fields
            rows[r : r + d.fields, :] = piece(cc, e)


def build_tables(d, trig, fwd, back):
    tall, fine = 3 * d.kc // 16, 16
    short = d.half // 16

    def turn(big, small):
        cb, sb, cs, ss = trig[0, big], trig[1, big], trig[0, small], trig[1, small]
        return cb * cs - sb * ss, -(sb * cs + cb * ss)

    for p in range(2):
        ramp = (2 * lax.broadcasted_iota(jnp.int32, (1, d.half), 1) + p).astype(F32) * (1.0 / d.modes)

        def ahead(a, _):
            cos, sin = turn(pl.ds(p * tall + a, 1), pl.ds((2 * tall + short + p * fine), fine))
            inside = lax.broadcasted_iota(jnp.int32, (fine, 1), 0) + a * fine <= d.half
            cos, sin = jnp.where(inside, cos, 0.0), jnp.where(inside, sin, 0.0)
            c = a // (d.kc // 16)
            at = (a - c * (d.kc // 16)) * 16
            for cc, pair in enumerate(((cos, ramp * sin), (sin, -ramp * cos))):
                for v, t in enumerate(pair):
                    top = t.astype(BF16)
                    fwd[p, cc, c, pl.ds(pl.multiple_of(2 * v * d.kc + at, 16), 16)] = top
                    fwd[p, cc, c, pl.ds(pl.multiple_of((2 * v + 1) * d.kc + at, 16), 16)] = (
                        t - top.astype(F32)
                    ).astype(BF16)
            return _

        lax.fori_loop(0, tall, ahead, None)
        first = jnp.where(lax.broadcasted_iota(jnp.int32, (1, d.half), 1) == 0, 0.5, 1.0)

        def behind(a, _):
            pair = turn(pl.ds(2 * tall + a, 1), pl.ds(2 * tall + short + (2 + p) * fine, fine))
            for cc, t in enumerate(pair):
                t = t * first
                top = t.astype(BF16)
                at = pl.multiple_of(a * 16, 16)
                back[p, cc, pl.ds(at, 16)] = top
                back[p, cc, pl.ds(pl.multiple_of(d.half + at, 16), 16)] = (t - top.astype(F32)).astype(BF16)
            return _

        lax.fori_loop(0, short, behind, None)


def trig_rows(d):
    points = 2 * d.modes
    tall, short = 3 * d.kc // 16, d.half // 16
    wave = 2 * np.arange(d.half)
    k = np.arange(d.half)
    big = [16 * np.arange(tall)[:, None] * (wave + p)[None] for p in range(2)]
    big.append(32 * np.arange(short)[:, None] * k[None])
    small = [np.arange(16)[:, None] * (wave + p)[None] for p in range(2)]
    small += [(2 * np.arange(16) + p)[:, None] * k[None] for p in range(2)]
    angle = np.concatenate(big + small) % points * (2.0 * np.pi / points)
    scale = np.where(np.arange(len(angle)) < 2 * tall + short, d.modes**-0.5, 1.0)[:, None]
    return np.stack([np.cos(angle) * scale, np.sin(angle) * scale]).astype(np.float32)


def synthesis_kernel(
    d, it_hbm, leg_hbm, trig, out, fwd_hbm, back_hbm, raw, rows, leg, stage, send, fwd, back,
    leg_sem, send_sem, recv_sem, own_sem, tab_sem,
):
    me = lax.axis_index("band")
    n, half, per = d.n, d.degrees // 2, d.mc // 2
    subs = d.mc // SUB
    peers = [lax.rem(me + off, n) for off in range(1, n)]
    greet("band", peers)

    def fetch(i, slot):
        return [
            pltpu.make_async_copy(leg_hbm.at[pl.ds(i * SUB, SUB)], leg.at[slot], leg_sem.at[slot, 0]),
            pltpu.make_async_copy(it_hbm.at[0, :, pl.ds(i * SUB, SUB)], raw.at[slot], leg_sem.at[slot, 1]),
        ]

    def remote(c, off):
        peer = lax.rem(me + off, n)
        return pltpu.make_async_remote_copy(
            src_ref=send.at[c, peer],
            dst_ref=out.at[:, me, pl.ds(c * per, per)],
            send_sem=send_sem.at[c, off],
            recv_sem=recv_sem.at[c, off],
            device_id={"band": peer},
            device_id_type=MESH,
        )

    def local(c):
        return pltpu.make_async_copy(
            send.at[c, me], out.at[:, me, pl.ds(c * per, per)], own_sem.at[c]
        )

    for copy_in in fetch(0, 0):
        copy_in.start()

    def chunk(c, _):
        def sub(j, _):
            i = c * subs + j
            slot = lax.rem(i, 2)

            @pl.when(i + 1 < d.nc * subs)
            def _():
                for copy_in in fetch(i + 1, 1 - slot):
                    copy_in.start()

            for copy_in in fetch(i, slot):
                copy_in.wait()
            for mi in range(SUB):
                gather_rows(d, rows.at[mi], lambda cc, e: raw[slot, cc, mi, e])
            for mi in range(SUB):
                x = rows[mi].astype(BF16)
                table = leg[slot, mi]
                for par in range(2):
                    cols = slice(par * half, (par + 1) * half)
                    y = mul(x[:, cols], table[:, cols], ((1,), (1,)))
                    for lb in range(d.nlb):
                        at = (lb * 2 + par) * d.rows * d.mc + (mi % 2) * per + j * (SUB // 2) + mi // 2
                        stage[pl.ds(at, d.rows, stride=d.mc), :] = y[:, lb * LANES : (lb + 1) * LANES]
            return _

        lax.fori_loop(0, subs, sub, None)
        for s in range(d.el):
            for f in range(d.fields):
                for p in range(2):
                    for cc in range(2):
                        g = ((s * d.fields + f) * 2 + p) * 2 + cc
                        for lb in range(d.nlb):
                            for eg in range(d.eg):
                                r = (cc * d.members + eg * d.el + s) * d.fields + f
                                tiles = [
                                    stage[pl.ds(((lb * 2 + par) * d.rows + r) * d.mc + p * per, per), :]
                                    for par in range(2)
                                ]
                                send[c, lb * d.eg + eg, g] = jnp.concatenate(tiles, axis=1).astype(BF16)
        for off in range(1, n):
            remote(c, off).start()
        local(c).start()
        return _

    lax.fori_loop(0, d.nc, chunk, None)
    build_tables(d, trig, fwd, back)
    saves = [
        pltpu.make_async_copy(fwd, fwd_hbm, tab_sem.at[0]),
        pltpu.make_async_copy(back, back_hbm, tab_sem.at[1]),
    ]
    for save in saves:
        save.start()

    def finish(c, _):
        for off in range(1, n):
            remote(c, off).wait()
        local(c).wait()
        return _

    lax.fori_loop(0, d.nc, finish, None)
    for save in saves:
        save.wait()


def synthesis(d, iterate, legendre, trig):
    blocks = d.el * d.g
    fwd = (2, 2, 3, 4 * d.kc, d.half)
    back = (2, 2, 2 * d.half, d.half)
    anywhere = pl.BlockSpec(memory_space=pl.ANY)
    return pl.pallas_call(
        functools.partial(synthesis_kernel, d),
        name="synthesis",
        out_shape=(
            jax.ShapeDtypeStruct((blocks, d.n, d.pl, 2 * d.lb), BF16),
            jax.ShapeDtypeStruct(fwd, BF16),
            jax.ShapeDtypeStruct(back, BF16),
        ),
        in_specs=[anywhere, anywhere, pl.BlockSpec(memory_space=pltpu.VMEM)],
        out_specs=(anywhere,) * 3,
        scratch_shapes=[
            pltpu.VMEM((2, 2, SUB, d.members, d.fields, d.degrees), F32),
            pltpu.VMEM((SUB, d.rows, d.degrees), F32),
            pltpu.VMEM((2, SUB, d.hemi, d.degrees), BF16),
            pltpu.VMEM((2 * d.nlb * d.rows * d.mc, LANES), F32),
            pltpu.VMEM((d.nc, d.n, blocks, d.mc // 2, 2 * d.lb), BF16),
            pltpu.VMEM(fwd, BF16),
            pltpu.VMEM(back, BF16),
            pltpu.SemaphoreType.DMA((2, 2)),
            pltpu.SemaphoreType.DMA((d.nc, d.n)),
            pltpu.SemaphoreType.DMA((d.nc, d.n)),
            pltpu.SemaphoreType.DMA((d.nc,)),
            pltpu.SemaphoreType.DMA((2,)),
        ],
        compiler_params=pltpu.CompilerParams(
            collective_id=1, has_side_effects=True, vmem_limit_bytes=VMEM_BYTES
        ),
    )(iterate, legendre, trig)


def four_points(ce, se, co, so):
    a, b, c, e = ce + se, ce - se, co + so, co - so
    return a + c, b + e, a - c, b - e


def fold_points(t):
    s13, s24, d13, d24 = t[0] + t[2], t[1] + t[3], t[0] - t[2], t[1] - t[3]
    return s13 + s24, s13 - s24, d13 + d24, d13 - d24


def grid_kernel(
    d, x_hbm, fwd_hbm, back_hbm, cor, weight, out, x, fwd, back, part, high, low, edge, send,
    x_sem, tab_sem, send_sem, recv_sem, own_sem,
):
    me = lax.axis_index("band")
    n, kc, lb, g = d.n, d.kc, d.lb, d.g
    peers = [lax.rem(me + off, n) for off in range(1, n)]

    def fetch(s):
        return pltpu.make_async_copy(x_hbm.at[pl.ds(s * g, g)], x.at[lax.rem(s, 2)], x_sem.at[lax.rem(s, 2)])

    tables = [
        pltpu.make_async_copy(fwd_hbm, fwd, tab_sem.at[0]),
        pltpu.make_async_copy(back_hbm, back, tab_sem.at[1]),
    ]
    fetch(0).start()
    for t in tables:
        t.start()
    greet("band", peers)

    def remote(s, f, off):
        peer = lax.rem(me + off, n)
        return pltpu.make_async_remote_copy(
            src_ref=send.at[pl.ds(s * g + f * 4, 4), pl.ds(peer * d.pl, d.pl)],
            dst_ref=out.at[s, me, pl.ds(f * 4, 4)],
            send_sem=send_sem.at[s * d.fields + f, off],
            recv_sem=recv_sem.at[s * d.fields + f, off],
            device_id={"band": peer},
            device_id_type=MESH,
        )

    def local(s, f):
        return pltpu.make_async_copy(
            send.at[pl.ds(s * g + f * 4, 4), pl.ds(me * d.pl, d.pl)],
            out.at[s, me, pl.ds(f * 4, 4)],
            own_sem.at[s * d.fields + f],
        )

    for t in tables:
        t.wait()

    def step(s, _):
        slot = lax.rem(s, 2)

        @pl.when(s + 1 < d.el)
        def _():
            fetch(s + 1).start()

        fetch(s).wait()

        def rows(c, _):
            def field(f, _):
                for p in range(2):
                    for cc in range(2):
                        q = p * 2 + cc
                        part[f * 4 + q] = mul(fwd[p, cc, c], x[slot, f * 4 + q], ((1,), (0,)))
                return _

            lax.fori_loop(0, d.fields, field, None)

            def block(i, _):
                def load(f, q, v):
                    return part[f * 4 + q, pl.ds(2 * v * kc + i * 16, 16)] + part[
                        f * 4 + q, pl.ds((2 * v + 1) * kc + i * 16, 16)
                    ]

                folded = []
                comps = [[[load(f, q, v) for q in range(4)] for v in range(2)] for f in range(d.fields)]
                for h in range(2):
                    val, slo = [], []
                    for f in range(d.fields):
                        hemi = [
                            [a[:, :lb] + a[:, lb:] if h == 0 else a[:, :lb] - a[:, lb:] for a in comps[f][v]]
                            for v in range(2)
                        ]
                        val.append(four_points(*hemi[0]))
                        g0, g1, g2, g3 = hemi[1]
                        slo.append(four_points(g1, g0, g3, g2))
                    c_lat = cor[h : h + 1]
                    tend = [[], [], []]
                    for k in range(4):
                        u, w, z = (val[f][k] for f in range(3))
                        du, dw, dz = (slo[f][k] for f in range(3))
                        tend[0].append(c_lat * w - u * du - dz)
                        tend[1].append(-u * dw - c_lat * u)
                        tend[2].append(-u * dz - (1.0 + z) * du)
                    folded.append([fold_points(t) for t in tend])
                at = pl.multiple_of(c * kc + i * 16, 16)
                for f in range(d.fields):
                    for q in range(4):
                        north, south = folded[0][f][q], folded[1][f][q]
                        t = jnp.concatenate([north + south, north - south], axis=1)
                        top = t.astype(BF16)
                        high[f * 4 + q, pl.ds(at, 16)] = top
                        low[f * 4 + q, pl.ds(at, 16)] = (t - top.astype(F32)).astype(BF16)
                        edge[f * 4 + q] = t[:8]
                return _

            lax.fori_loop(0, kc // 16, block, None)
            return _

        lax.fori_loop(0, 3, rows, None)

        def field(f, _):
            for q in range(4):
                p, cc = divmod(q, 2)
                both = mul(back[p, cc], high[f * 4 + q, : d.half], ((1,), (0,)))
                spec = both[: d.half] + both[d.half :]
                spec = spec + mul(back[p, cc, : d.half], low[f * 4 + q, : d.half], ((1,), (0,)))
                if p == cc:
                    sign = 1.0 - 2.0 * (lax.broadcasted_iota(jnp.int32, (d.half, 1), 0) % 2).astype(F32)
                    scale = 0.5 / math.sqrt(d.modes) * (1.0 if p == 0 else -1.0)
                    spec = spec + (sign * scale) * edge[f * 4 + q, :1]
                send[s * g + f * 4 + q] = (spec * weight[...]).astype(BF16)
            for off in range(1, n):
                remote(s, f, off).start()
            local(s, f).start()
            return _

        lax.fori_loop(0, d.fields, field, None)
        return _

    lax.fori_loop(0, d.el, step, None)

    def finish(i, _):
        s, f = i // d.fields, i % d.fields
        for off in range(1, n):
            remote(s, f, off).wait()
        local(s, f).wait()
        return _

    lax.fori_loop(0, d.el * d.fields, finish, None)


def grid_step(d, x, fwd, back, cor, weight):
    anywhere = pl.BlockSpec(memory_space=pl.ANY)
    vmem = pl.BlockSpec(memory_space=pltpu.VMEM)
    n, g = d.n, d.g
    return pl.pallas_call(
        functools.partial(grid_kernel, d),
        name="grid",
        out_shape=jax.ShapeDtypeStruct((d.el, n, g, d.pl, 2 * d.lb), BF16),
        in_specs=[anywhere, anywhere, anywhere, vmem, vmem],
        out_specs=anywhere,
        scratch_shapes=[
            pltpu.VMEM((2, g, d.half, 2 * d.lb), BF16),
            pltpu.VMEM(fwd.shape, BF16),
            pltpu.VMEM(back.shape, BF16),
            pltpu.VMEM((g, 4 * d.kc, 2 * d.lb), F32),
            pltpu.VMEM((g, 3 * d.kc, 2 * d.lb), BF16),
            pltpu.VMEM((g, 3 * d.kc, 2 * d.lb), BF16),
            pltpu.VMEM((g, 8, 2 * d.lb), F32),
            pltpu.VMEM((d.el * g, d.half, 2 * d.lb), BF16),
            pltpu.SemaphoreType.DMA((2,)),
            pltpu.SemaphoreType.DMA((2,)),
            pltpu.SemaphoreType.DMA((d.el * d.fields, n)),
            pltpu.SemaphoreType.DMA((d.el * d.fields, n)),
            pltpu.SemaphoreType.DMA((d.el * d.fields,)),
        ],
        compiler_params=pltpu.CompilerParams(
            collective_id=2, has_side_effects=True, vmem_limit_bytes=VMEM_BYTES
        ),
    )(x, fwd, back, cor, weight)


def analysis_kernel(
    d, spectra, leg_hbm, state_hbm, spec_hbm, rate_hbm, quad, out, total_out,
    leg, raw, damp, drift, recv, lhs, own, outer, cross, far, partial, bufs, rates, mix_rows, result, sums,
    norms, band_norms, node_norms,
    leg_sem, recv_sem, own_send, fwd_send, par_send, o_sem, x_sem, y_sem, buf_sem, res_sem, norm_sem,
):
    node = lax.axis_index("node")
    band = lax.axis_index("band")
    half, per, subs = d.degrees // 2, d.mc // 2, d.mc // SUB
    total = d.nc * subs
    is_outer = lax.rem(node, 3) == 0
    beside = jnp.where(is_outer, 1 + node // 3, (node - 1) * 3)
    other = jnp.where(is_outer, beside, 3 - node)
    far_node = jnp.where(is_outer, 0, 3 - beside)

    near = [("band", lax.rem(band + off, d.n)) for off in range(1, d.n)]
    near += [("node", lax.rem(node + off, d.nnode)) for off in range(1, d.nnode)]
    sem = pltpu.get_barrier_semaphore()
    for axis, peer in near:
        pl.semaphore_signal(sem, inc=1, device_id={axis: peer}, device_id_type=MESH)
    pl.semaphore_wait(sem, len(near))

    def copy(src, dst, send, recv_s, c, peer):
        return pltpu.make_async_remote_copy(
            src_ref=src.at[c], dst_ref=dst.at[c], send_sem=send.at[c], recv_sem=recv_s.at[c],
            device_id={"node": peer}, device_id_type=MESH,
        )

    def to_inner(c):
        return copy(own, outer, own_send, o_sem, c, beside)

    def to_other(c):
        return copy(own, cross, own_send, x_sem, c, other)

    def forward(c):
        return copy(outer, far, fwd_send, y_sem, c, other)

    def to_outer(c):
        return copy(partial, cross, par_send, x_sem, c, beside)

    def fetch(i, slot):
        return [
            pltpu.make_async_copy(leg_hbm.at[pl.ds(i * SUB, SUB)], leg.at[slot], leg_sem.at[slot, 0]),
            pltpu.make_async_copy(spec_hbm.at[0, :, pl.ds(i * SUB, SUB)], raw.at[slot, 0], leg_sem.at[slot, 1]),
            pltpu.make_async_copy(state_hbm.at[:, pl.ds(i * SUB, SUB)], raw.at[slot, 1], leg_sem.at[slot, 2]),
            pltpu.make_async_copy(rate_hbm.at[pl.ds(i * SUB, SUB)], damp.at[slot], leg_sem.at[slot, 3]),
        ]

    def fetch_spectra(c, slot):
        return pltpu.make_async_copy(
            spectra.at[:, :, :, pl.ds(c * per, per)], recv.at[slot], recv_sem.at[slot]
        )

    for copy_in in fetch(0, 0):
        copy_in.start()
    fetch_spectra(0, 0).start()

    def chunk(c, _):
        cslot = lax.rem(c, 2)

        @pl.when(c + 1 < d.nc)
        def _():
            fetch_spectra(c + 1, 1 - cslot).start()

        fetch_spectra(c, cslot).wait()
        for s in range(d.el):
            for lb in range(d.nlb):
                for eg in range(d.eg):
                    for f in range(d.fields):
                        for p in range(2):
                            for cc in range(2):
                                r = (cc * d.members + eg * d.el + s) * d.fields + f
                                tile = recv[cslot, s, lb * d.eg + eg, f * 4 + p * 2 + cc].astype(F32)
                                for par in range(2):
                                    at = ((par * d.nlb + lb) * d.rows + r) * d.mc + p * per
                                    lhs[pl.ds(at, per), :] = tile[:, par * d.lb : (par + 1) * d.lb]

        def sub(j, _):
            i = c * subs + j
            slot = lax.rem(i, 2)

            @pl.when(i + 1 < total)
            def _():
                for copy_in in fetch(i + 1, 1 - slot):
                    copy_in.start()

            for copy_in in fetch(i, slot):
                copy_in.wait()
            for mi in range(SUB):
                gather_rows(
                    d,
                    drift.at[mi],
                    lambda cc, e: damp[slot, mi] * (raw[slot, 0, cc, mi, e] - raw[slot, 1, cc, mi, e]),
                )
            for mi in range(SUB):
                for par in range(2):
                    pieces = [
                        lhs[
                            pl.ds(
                                (par * d.nlb + lb) * d.rows * d.mc + (mi % 2) * per + j * (SUB // 2) + mi // 2,
                                d.rows,
                                stride=d.mc,
                            ),
                            :,
                        ]
                        for lb in range(d.nlb)
                    ]
                    rows = jnp.concatenate(pieces, axis=1).astype(BF16)
                    cols = slice(par * half, (par + 1) * half)
                    y = mul(rows, leg[slot, mi, :, cols], ((1,), (0,)))
                    own[c, j * SUB + mi, :, cols] = (y - drift[mi, :, cols]).astype(BF16)
            return _

        lax.fori_loop(0, subs, sub, None)

        @pl.when(is_outer)
        def _():
            to_inner(c).start()

        @pl.when(jnp.logical_not(is_outer))
        def _():
            to_other(c).start()

            @pl.when(c >= 1)
            def _():
                to_inner(c - 1).wait_recv()
                forward(c - 1).start()

        return _

    lax.fori_loop(0, d.nc, chunk, None)

    @pl.when(jnp.logical_not(is_outer))
    def _():
        to_inner(d.nc - 1).wait_recv()
        forward(d.nc - 1).start()

    def load(c, slot):
        at = pl.ds(c * d.mc, d.mc)
        return [
            pltpu.make_async_copy(state_hbm.at[:, at], bufs.at[slot, 0], buf_sem.at[slot, 0]),
            pltpu.make_async_copy(spec_hbm.at[0, :, at], bufs.at[slot, 1], buf_sem.at[slot, 1]),
            pltpu.make_async_copy(rate_hbm.at[at], rates.at[slot], buf_sem.at[slot, 2]),
        ]

    def save(c, slot):
        return pltpu.make_async_copy(result.at[slot], out.at[0, :, pl.ds(c * d.mc, d.mc)], res_sem.at[slot])

    for copy_in in load(0, 0):
        copy_in.start()
    sums[...] = jnp.zeros_like(sums)
    q_own = quad[node, node]
    q_total = quad[node, 0] + quad[node, 1] + quad[node, 2] + quad[node, 3]

    def combine(c, _):
        slot = lax.rem(c, 2)

        @pl.when(c + 1 < d.nc)
        def _():
            for copy_in in load(c + 1, 1 - slot):
                copy_in.start()

        for copy_in in load(c, slot):
            copy_in.wait()

        @pl.when(c >= 2)
        def _():
            save(c - 2, slot).wait()

        @pl.when(jnp.logical_not(is_outer))
        def _():
            to_other(c).wait_recv()
            forward(c).wait_recv()

            def mode(m, _):
                a, b = own[c, m].astype(F32), cross[c, m].astype(F32)
                o, y = outer[c, m].astype(F32), far[c, m].astype(F32)
                mix = quad[beside, node] * a + quad[beside, other] * b + quad[beside, far_node] * y
                partial[c, m] = mix.astype(BF16)
                mix_rows[m] = (
                    q_own * a + quad[node, other] * b + quad[node, beside] * o + quad[node, far_node] * y
                )
                return _

            lax.fori_loop(0, d.mc, mode, None)
            to_outer(c).start()

        @pl.when(is_outer)
        def _():
            to_outer(c).wait_recv()

            def mode(m, _):
                mix_rows[m] = q_own * own[c, m].astype(F32) + cross[c, m].astype(F32)
                return _

            lax.fori_loop(0, d.mc, mode, None)

        def update(m, _):
            rate = rates[slot, m]
            scale = q_own * rate
            below = 1.0 + scale
            changed, start = jnp.zeros_like(rate), jnp.zeros_like(rate)
            for cc in range(2):
                for e in range(d.members):
                    r = (cc * d.members + e) * d.fields
                    state, spec = bufs[slot, 0, cc, m, e], bufs[slot, 1, cc, m, e]
                    mixed = mix_rows[m, r : r + d.fields, :] - q_total * (rate * state)
                    new = (state + mixed + scale * spec) / below
                    result[slot, cc, m, e] = new
                    changed += (new - spec) * (new - spec)
                    start += state * state
            sums[0] += changed
            sums[1] += start
            return _

        lax.fori_loop(0, d.mc, update, None)
        save(c, slot).start()
        return _

    lax.fori_loop(0, d.nc, combine, None)
    for c in range(max(d.nc - 2, 0), d.nc):
        save(c, c % 2).wait()

    def finish(c, _):
        @pl.when(is_outer)
        def _():
            to_inner(c).wait_send()

        @pl.when(jnp.logical_not(is_outer))
        def _():
            to_other(c).wait_send()
            forward(c).wait_send()
            to_outer(c).wait_send()

        return _

    lax.fori_loop(0, d.nc, finish, None)

    def spread(axis, me, count, slots, k):
        slots[me] = norms[k]
        copies = [
            pltpu.make_async_remote_copy(
                src_ref=norms.at[k], dst_ref=slots.at[me],
                send_sem=norm_sem.at[k, 0, off], recv_sem=norm_sem.at[k, 1, off],
                device_id={axis: lax.rem(me + off, count)}, device_id_type=MESH,
            )
            for off in range(1, count)
        ]
        for each in copies:
            each.start()
        for each in copies:
            each.wait()
        return sum(slots[i] for i in range(count))

    flat = sum(sums[:, :, k : k + LANES] for k in range(0, d.degrees, LANES))
    norms[...] = jnp.zeros_like(norms)
    for v in range(2):
        norms[0, 4 * v : 4 * v + d.fields, :] = flat[v]
    norms[1] = spread("band", band, d.n, band_norms, 0)
    total_out[...] = spread("node", node, d.nnode, node_norms, 1)


def analysis(d, spectra, legendre, state, iterate, rate, quadrature):
    anywhere = pl.BlockSpec(memory_space=pl.ANY)
    natural = (2, d.mc, d.members, d.fields, d.degrees)
    block = pltpu.VMEM((d.nc, d.mc, d.rows, d.degrees), BF16)
    dma = pltpu.SemaphoreType.DMA
    return pl.pallas_call(
        functools.partial(analysis_kernel, d),
        name="analysis",
        out_shape=(
            jax.ShapeDtypeStruct(iterate.shape, F32),
            jax.ShapeDtypeStruct((8, LANES), F32),
        ),
        in_specs=[anywhere] * 5 + [pl.BlockSpec(memory_space=pltpu.SMEM)],
        out_specs=(anywhere, pl.BlockSpec(memory_space=pltpu.VMEM)),
        scratch_shapes=[
            pltpu.VMEM((2, SUB, d.hemi, d.degrees), BF16),
            pltpu.VMEM((2, 2, 2, SUB, d.members, d.fields, d.degrees), F32),
            pltpu.VMEM((2, SUB, d.fields, d.degrees), F32),
            pltpu.VMEM((SUB, d.rows, d.degrees), F32),
            pltpu.VMEM((2, d.el, d.n, d.g, d.mc // 2, 2 * d.lb), BF16),
            pltpu.VMEM((2 * d.nlb * d.rows * d.mc, LANES), F32),
            block,
            block,
            block,
            block,
            block,
            pltpu.VMEM((2, 2) + natural, F32),
            pltpu.VMEM((2, d.mc, d.fields, d.degrees), F32),
            pltpu.VMEM((d.mc, d.rows, d.degrees), F32),
            pltpu.VMEM((2,) + natural, F32),
            pltpu.VMEM((2, d.fields, d.degrees), F32),
            pltpu.VMEM((2, 8, LANES), F32),
            pltpu.VMEM((d.n, 8, LANES), F32),
            pltpu.VMEM((d.nnode, 8, LANES), F32),
            dma((2, 4)),
            dma((2,)),
            dma((d.nc,)),
            dma((d.nc,)),
            dma((d.nc,)),
            dma((d.nc,)),
            dma((d.nc,)),
            dma((d.nc,)),
            dma((2, 3)),
            dma((2,)),
            dma((2, 2, d.n)),
        ],
        compiler_params=pltpu.CompilerParams(
            collective_id=3, has_side_effects=True, vmem_limit_bytes=VMEM_BYTES
        ),
    )(spectra, legendre, state, iterate, rate, quadrature)


def fast_body(d, state0, iterate, legendre, lat_weight, coriolis, damping, quadrature):
    band = lax.axis_index("band")
    first = (band // d.eg) * d.lb
    cor = lax.dynamic_slice_in_dim(coriolis, first, d.lb, 1)
    weight = jnp.tile(lax.dynamic_slice_in_dim(lat_weight, first, d.lb, 0), 2)[None]
    x, forward, back = synthesis(d, iterate, legendre, jnp.asarray(trig_rows(d)))
    x = x.reshape(d.el * d.g, d.half, 2 * d.lb)
    spectra = grid_step(d, x, forward, back, cor, weight)
    updated, norms = analysis(d, spectra, legendre, state0, iterate, damping, quadrature)
    total = norms.reshape(2, 4, LANES)[:, : d.fields].sum(axis=2)
    return updated, jnp.sqrt(total[0] / (total[1] + 1e-06))


def solution(mesh):
    placed = (
        P(None, "band", None, None, None),
        P("node", None, "band", None, None, None),
        P("band", None, None),
        P(),
        P(),
        P("band", None, None),
        P(),
    )

    def call(*args):
        d = Plan(mesh.shape["band"], mesh.shape["node"], args[1].shape, args[2].shape)
        body = functools.partial(fast_body, d) if d.fits else plain_body
        return jax.shard_map(
            body,
            mesh=mesh,
            in_specs=placed,
            out_specs=(P("node", None, "band", None, None, None), P()),
            check_vma=False,
        )(*args)

    return call
```

```python
import functools
import math

import jax
import jax.numpy as jnp
import numpy as np
from jax import lax
from jax.experimental import pallas as pl
from jax.experimental.pallas import tpu as pltpu
from jax.sharding import PartitionSpec as P

MESH = pl.DeviceIdType.MESH
F32, BF16 = jnp.float32, jnp.bfloat16
VMEM_BYTES = 63_000_000
LANES = 128
SUB = 4


def split_bf16(x):
    high = lax.reduce_precision(x, 8, 7)
    return high.astype(jnp.bfloat16), (x - high).astype(jnp.bfloat16)


def dft_table(parity, nband, local_modes, modes, points):
    fine = 32
    coarse = modes // fine
    column = lax.iota(jnp.int32, modes)
    pairs = local_modes // 2
    part = column // pairs % 2
    wave = column // local_modes * local_modes + column % pairs * 2 + parity
    unit = 2.0 * math.pi / points

    def angle(index):
        return (index % points).astype(jnp.float32) * unit

    big = angle(
        lax.iota(jnp.int32, coarse)[:, None] * fine * wave[None] + part[None] * (points // 4)
    )
    small = angle(lax.iota(jnp.int32, fine)[:, None] * wave[None])
    cos_big, sin_big = jnp.cos(big)[:, None], jnp.sin(big)[:, None]
    cos_small, sin_small = jnp.cos(small)[None], jnp.sin(small)[None]
    scale = 1.0 / math.sqrt(modes)
    slope_scale = wave.astype(jnp.float32) * (scale / modes)
    value = (cos_big * cos_small - sin_big * sin_small).reshape(modes, modes) * scale
    slope = -(sin_big * cos_small + cos_big * sin_small).reshape(modes, modes) * slope_scale
    return split_bf16(value), split_bf16(slope)


def mul(a, b, dims):
    return lax.dot_general(a, b, (dims, ((), ())), preferred_element_type=jnp.float32)


def plain_body(state0, iterate, legendre, lat_weight, coriolis, damping, quadrature):
    spec = iterate[0]
    degrees = legendre.shape[2]
    half = degrees // 2
    local_modes, hemi = legendre.shape[:2]
    members, fields = spec.shape[2:4]
    nband = lax.axis_size("band")
    nnode = lax.axis_size("node")
    modes = local_modes * nband
    points = 2 * modes
    pairs = local_modes // 2
    lat_rows = hemi // nband
    node = lax.axis_index("node")
    band = lax.axis_index("band")
    tables = [dft_table(p, nband, local_modes, modes, points) for p in range(2)]
    cor = lax.dynamic_slice_in_dim(coriolis, band * lat_rows, lat_rows, 1)
    weight = lax.dynamic_slice_in_dim(lat_weight, band * lat_rows, lat_rows, 0)
    quad_row = lax.dynamic_slice_in_dim(quadrature, node, 1, 0)[0]
    diag = lax.dynamic_slice(quadrature, (node, node), (1, 1))[0, 0]
    is_even = lax.iota(jnp.int32, degrees) < half
    rate = damping[None, :, None]

    groups = 2
    ens = members // groups

    def synthesis(first):
        coeff = spec[:, :, first : first + ens].astype(jnp.bfloat16)
        coeff = coeff.transpose(1, 0, 3, 2, 4)
        zero = jnp.zeros((), jnp.bfloat16)
        rows = jnp.stack([jnp.where(is_even, coeff, zero), jnp.where(is_even, zero, coeff)], axis=1)
        rows = rows.reshape(local_modes, 4 * fields * ens, degrees)
        four = jnp.einsum("mrj,mlj->mrl", rows, legendre, preferred_element_type=jnp.float32)
        four = four.astype(jnp.bfloat16)
        four = four.reshape(pairs, 2, 2, 2, fields, ens, nband, lat_rows)
        four = four.transpose(6, 1, 3, 0, 2, 4, 5, 7)
        four = four.reshape(nband, 2, 2, pairs, 2 * fields * ens * lat_rows)
        return lax.all_to_all(four, "band", split_axis=0, concat_axis=0, tiled=True)

    def grid_step(four):
        shape = (modes, 2, fields, ens * lat_rows)
        parts = []
        for p in range(2):
            x = four[:, p].reshape(modes, -1)
            pair = []
            for high, low in tables[p]:
                dims = ((1,), (0,))
                pair.append((mul(high, x, dims) + mul(low, x, dims)).reshape(shape))
            parts.append(pair)
        tends = []
        for h in range(2):
            value, slope = (
                parts[0][v] + parts[1][v] if h == 0 else parts[0][v] - parts[1][v] for v in range(2)
            )
            hemis = []
            for s in range(2):
                val, slo = (
                    g[:, 0] + g[:, 1] if s == 0 else g[:, 0] - g[:, 1] for g in (value, slope)
                )
                c = jnp.tile(cor[s], ens)
                u, v, z = (val[:, f] for f in range(3))
                du, dv, dz = (slo[:, f] for f in range(3))
                hemis.append(
                    jnp.stack(
                        [-u * du + c * v - dz, -u * dv - c * u, -u * dz - (1.0 + z) * du], axis=1
                    )
                )
            tends.append(jnp.stack([hemis[0] + hemis[1], hemis[0] - hemis[1]], axis=1))
        scale = jnp.tile(weight, 2 * fields * ens)
        spectra = []
        for p in range(2):
            z = tends[0] + tends[1] if p == 0 else tends[0] - tends[1]
            zh, zl = split_bf16(z.reshape(modes, -1))
            high, low = tables[p][0]
            dims = ((0,), (0,))
            s = mul(high, zh, dims) + mul(high, zl, dims) + mul(low, zh, dims)
            spectra.append((s * scale).astype(jnp.bfloat16).reshape(nband, 2, pairs, -1))
        out = jnp.stack(spectra, axis=1)
        return lax.all_to_all(out, "band", split_axis=0, concat_axis=0, tiled=True)

    def analysis(out, first):
        out = out.reshape(nband, 2, 2, pairs, 2, fields, ens, lat_rows)
        out = out.transpose(3, 1, 4, 2, 5, 6, 0, 7)
        out = out.reshape(local_modes, 4 * fields * ens, hemi)
        both = jnp.einsum("mrl,mlj->mrj", out, legendre, preferred_element_type=jnp.float32)
        both = both.reshape(local_modes, 2, 2, fields, ens, degrees)
        nonlinear = jnp.where(is_even, both[:, 0], both[:, 1]).transpose(1, 0, 3, 2, 4)
        part = slice(first, first + ens)
        rest = nonlinear - rate * (spec[:, :, part] - state0[:, :, part])
        gathered = lax.all_gather(rest.astype(jnp.bfloat16), "node")
        mixed = sum(quad_row[p] * gathered[p].astype(jnp.float32) for p in range(nnode))
        return mixed

    received = [synthesis(g * ens) for g in range(groups)]
    spectra = [grid_step(r) for r in received]
    mixed = [analysis(s, g * ens) for g, s in enumerate(spectra)]
    mixed = jnp.concatenate(mixed, axis=2) - jnp.sum(quad_row) * (rate * state0)
    updated = (state0 + mixed + diag * rate * spec) / (1.0 + diag * rate)
    change = jnp.sum((updated - spec) ** 2, axis=(0, 1, 2, 4))
    base = jnp.sum(state0 * state0, axis=(0, 1, 2, 4))
    total = lax.psum(jnp.stack([change, base]), ("node", "band"))
    ratio = jnp.sqrt(total[0] / (total[1] + 1e-06))
    return (updated[None], ratio)


class Plan:
    def __init__(self, nband, nnode, iterate, legendre):
        self.n, self.nnode = nband, nnode
        self.modes, self.members, self.fields, self.degrees = iterate[2:]
        self.hemi = legendre[1]
        self.ml = self.modes // nband
        self.lb = LANES
        self.nlb = self.hemi // self.lb
        self.eg = max(nband // max(self.nlb, 1), 1)
        self.el = self.members // self.eg
        self.rows = 2 * self.members * self.fields
        self.pl = self.ml // 2
        self.mc = 16
        self.nc = self.ml // self.mc
        self.half = self.modes // 2
        self.kc = (self.half + 16) // 3
        self.g = 4 * self.fields
        self.fits = (
            nnode == 4
            and self.fields == 3
            and self.nlb * self.eg == nband
            and self.eg * self.el == self.members
            and self.hemi % self.lb == 0
            and self.ml % self.mc == 0
            and self.modes % nband == 0
            and (self.half + 16) % 48 == 0
            and self.rows % 8 == 0
            and self.degrees % 256 == 0
        )


def gather_rows(d, rows, piece):
    for cc in range(2):
        for f in range(d.fields):
            r = (cc * d.fields + f) * d.members
            rows[r : r + d.members, :] = piece(cc, f)


def build_tables(d, trig, fwd, back):
    tall, fine = 3 * d.kc // 16, 16
    short = d.half // 16

    def turn(big, small):
        cb, sb, cs, ss = trig[0, big], trig[1, big], trig[0, small], trig[1, small]
        return cb * cs - sb * ss, -(sb * cs + cb * ss)

    for p in range(2):
        ramp = (2 * lax.broadcasted_iota(jnp.int32, (1, d.half), 1) + p).astype(F32) * (1.0 / d.modes)

        def ahead(a, _):
            cos, sin = turn(pl.ds(p * tall + a, 1), pl.ds((2 * tall + short + p * fine), fine))
            inside = lax.broadcasted_iota(jnp.int32, (fine, 1), 0) + a * fine <= d.half
            cos, sin = jnp.where(inside, cos, 0.0), jnp.where(inside, sin, 0.0)
            c = a // (d.kc // 16)
            at = (a - c * (d.kc // 16)) * 16
            for cc, pair in enumerate(((cos, ramp * sin), (sin, -ramp * cos))):
                for v, t in enumerate(pair):
                    top = t.astype(BF16)
                    fwd[p, cc, c, pl.ds(pl.multiple_of(2 * v * d.kc + at, 16), 16)] = top
                    fwd[p, cc, c, pl.ds(pl.multiple_of((2 * v + 1) * d.kc + at, 16), 16)] = (
                        t - top.astype(F32)
                    ).astype(BF16)
            return _

        lax.fori_loop(0, tall, ahead, None)
        first = jnp.where(lax.broadcasted_iota(jnp.int32, (1, d.half), 1) == 0, 0.5, 1.0)

        def behind(a, _):
            pair = turn(pl.ds(2 * tall + a, 1), pl.ds(2 * tall + short + (2 + p) * fine, fine))
            for cc, t in enumerate(pair):
                t = t * first
                top = t.astype(BF16)
                at = pl.multiple_of(a * 16, 16)
                back[p, cc, pl.ds(at, 16)] = top
                back[p, cc, pl.ds(pl.multiple_of(d.half + at, 16), 16)] = (t - top.astype(F32)).astype(BF16)
            return _

        lax.fori_loop(0, short, behind, None)


def trig_rows(d):
    points = 2 * d.modes
    tall, short = 3 * d.kc // 16, d.half // 16
    wave = 2 * np.arange(d.half)
    k = np.arange(d.half)
    big = [16 * np.arange(tall)[:, None] * (wave + p)[None] for p in range(2)]
    big.append(32 * np.arange(short)[:, None] * k[None])
    small = [np.arange(16)[:, None] * (wave + p)[None] for p in range(2)]
    small += [(2 * np.arange(16) + p)[:, None] * k[None] for p in range(2)]
    angle = np.concatenate(big + small) % points * (2.0 * np.pi / points)
    scale = np.where(np.arange(len(angle)) < 2 * tall + short, d.modes**-0.5, 1.0)[:, None]
    return np.stack([np.cos(angle) * scale, np.sin(angle) * scale]).astype(np.float32)


def four_points(ce, se, co, so):
    a, b, c, e = ce + se, ce - se, co + so, co - so
    return a + c, b + e, a - c, b - e


def fold_points(t):
    s13, s24, d13, d24 = t[0] + t[2], t[1] + t[3], t[0] - t[2], t[1] - t[3]
    return s13 + s24, s13 - s24, d13 + d24, d13 - d24


def sweep_kernel(
    d, it_hbm, leg_hbm, state_hbm, rate_hbm, trig, cor, weight, quad,
    out, total_out, x_hbm, spectra,
    send, fwd, back, send_back, outer, cross, far, sums, norms, band_norms, node_norms,
    leg_sem, a_send, a_recv, a_own, x_sem, b_send, b_recv, b_own, recv_sem,
    own_send, fwd_send, par_send, o_sem, x_recv, y_sem, buf_sem, res_sem, norm_sem,
):
    band, node = lax.axis_index("band"), lax.axis_index("node")
    n, g, half = d.n, d.g, d.degrees // 2
    per, subs = d.mc // 2, d.mc // SUB
    total = d.nc * subs
    last = d.el - 1

    near = [("band", lax.rem(band + off, n)) for off in range(1, n)]
    near += [("node", lax.rem(node + off, d.nnode)) for off in range(1, d.nnode)]
    sem = pltpu.get_barrier_semaphore()
    for axis, peer in near:
        pl.semaphore_signal(sem, inc=1, device_id={axis: peer}, device_id_type=MESH)
    pl.semaphore_wait(sem, len(near))

    def ahead(s, c, off):
        peer = lax.rem(band + off, n)
        return pltpu.make_async_remote_copy(
            src_ref=send.at[c, s, peer],
            dst_ref=x_hbm.at[pl.ds(s * g, g), band, pl.ds(c * per, per)],
            send_sem=a_send.at[s * d.nc + c, off],
            recv_sem=a_recv.at[s * d.nc + c, off],
            device_id={"band": peer},
            device_id_type=MESH,
        )

    def ahead_own(s, c):
        return pltpu.make_async_copy(
            send.at[c, s, band], x_hbm.at[pl.ds(s * g, g), band, pl.ds(c * per, per)], a_own.at[s * d.nc + c]
        )

    def start_ahead(s, c):
        for off in range(1, n):
            ahead(s, c, off).start()
        ahead_own(s, c).start()

    def synthesis(raw, rows, leg, stage):
        def fetch(i, slot):
            return [
                pltpu.make_async_copy(leg_hbm.at[pl.ds(i * SUB, SUB)], leg.at[slot], leg_sem.at[slot, 0]),
                pltpu.make_async_copy(it_hbm.at[0, :, pl.ds(i * SUB, SUB)], raw.at[slot], leg_sem.at[slot, 1]),
            ]

        for copy_in in fetch(0, 0):
            copy_in.start()

        def chunk(c, _):
            def sub(j, _):
                i = c * subs + j
                slot = lax.rem(i, 2)

                @pl.when(i + 1 < total)
                def _():
                    for copy_in in fetch(i + 1, 1 - slot):
                        copy_in.start()

                for copy_in in fetch(i, slot):
                    copy_in.wait()
                for mi in range(SUB):
                    gather_rows(d, rows.at[mi], lambda cc, f: raw[slot, cc, mi, f])
                for mi in range(SUB):
                    x = rows[mi].astype(BF16)
                    table = leg[slot, mi]
                    for par in range(2):
                        cols = slice(par * half, (par + 1) * half)
                        y = mul(x[:, cols], table[:, cols], ((1,), (1,)))
                        for lb in range(d.nlb):
                            at = (lb * 2 + par) * d.rows * d.mc + (mi % 2) * per + j * (SUB // 2) + mi // 2
                            stage[pl.ds(at, d.rows, stride=d.mc), :] = y[:, lb * LANES : (lb + 1) * LANES]
                return _

            lax.fori_loop(0, subs, sub, None)
            for s in range(d.el):
                for f in range(d.fields):
                    for p in range(2):
                        for cc in range(2):
                            for lb in range(d.nlb):
                                for eg in range(d.eg):
                                    r = (cc * d.fields + f) * d.members + eg * d.el + s
                                    tiles = [
                                        stage[pl.ds(((lb * 2 + par) * d.rows + r) * d.mc + p * per, per), :]
                                        for par in range(2)
                                    ]
                                    send[c, s, lb * d.eg + eg, (f * 2 + p) * 2 + cc] = jnp.concatenate(
                                        tiles, axis=1
                                    ).astype(BF16)
            start_ahead(0, c)
            return _

        lax.fori_loop(0, d.nc, chunk, None)

    pl.run_scoped(
        synthesis,
        pltpu.VMEM((2, 2, SUB, d.fields, d.members, d.degrees), F32),
        pltpu.VMEM((SUB, d.rows, d.degrees), F32),
        pltpu.VMEM((2, SUB, d.hemi, d.degrees), BF16),
        pltpu.VMEM((2 * d.nlb * d.rows * d.mc, LANES), F32),
    )
    if d.el > 1:

        def rest(i, _):
            start_ahead(1 + i // d.nc, lax.rem(i, d.nc))
            return _

        lax.fori_loop(0, last * d.nc, rest, None)
    build_tables(d, trig, fwd, back)

    def behind(s, f, off):
        peer = lax.rem(band + off, n)
        k = s * d.fields + f
        return pltpu.make_async_remote_copy(
            src_ref=send_back.at[pl.ds(s * g + f * 4, 4), pl.ds(peer * d.pl, d.pl)],
            dst_ref=spectra.at[s, band, pl.ds(f * 4, 4)],
            send_sem=b_send.at[k, off],
            recv_sem=b_recv.at[k, off],
            device_id={"band": peer},
            device_id_type=MESH,
        )

    def behind_own(s, f):
        return pltpu.make_async_copy(
            send_back.at[pl.ds(s * g + f * 4, 4), pl.ds(band * d.pl, d.pl)],
            spectra.at[s, band, pl.ds(f * 4, 4)],
            b_own.at[s * d.fields + f],
        )

    def final(c, off):
        peer = lax.rem(band + off, n)
        k = last * d.fields + c
        return pltpu.make_async_remote_copy(
            src_ref=send_back.at[pl.ds(last * g, g), pl.ds(peer * d.pl + c * per, per)],
            dst_ref=spectra.at[last, band, :, pl.ds(c * per, per)],
            send_sem=b_send.at[k, off],
            recv_sem=b_recv.at[k, off],
            device_id={"band": peer},
            device_id_type=MESH,
        )

    def final_own(c):
        return pltpu.make_async_copy(
            send_back.at[pl.ds(last * g, g), pl.ds(band * d.pl + c * per, per)],
            spectra.at[last, band, :, pl.ds(c * per, per)],
            b_own.at[last * d.fields + c],
        )

    def grid(x, part, high, low, edge):
        kc, lb = d.kc, d.lb

        def step(s, _):
            def arrive(c, _):
                for off in range(1, n):
                    ahead(s, c, off).wait_recv()
                ahead_own(s, c).wait()
                return _

            lax.fori_loop(0, d.nc, arrive, None)
            fetch = pltpu.make_async_copy(x_hbm.at[pl.ds(s * g, g)], x, x_sem.at[0])
            fetch.start()
            fetch.wait()

            def rows(c, _):
                def field(f, _):
                    for p in range(2):
                        for cc in range(2):
                            q = p * 2 + cc
                            y = mul(fwd[p, cc, c], x[f * 4 + q].reshape(d.half, 2 * lb), ((1,), (0,)))
                            part[f * 4 + q, :kc] = y[:kc] + y[kc : 2 * kc]
                            part[f * 4 + q, kc:] = y[2 * kc : 3 * kc] + y[3 * kc :]
                    return _

                lax.fori_loop(0, d.fields, field, None)

                def block(i, _):
                    def load(f, q, v):
                        return part[f * 4 + q, pl.ds(pl.multiple_of(v * kc + i * 16, 16), 16)]

                    folded = []
                    comps = [[[load(f, q, v) for q in range(4)] for v in range(2)] for f in range(d.fields)]
                    for h in range(2):
                        val, slo = [], []
                        for f in range(d.fields):
                            hemi = [
                                [a[:, :lb] + a[:, lb:] if h == 0 else a[:, :lb] - a[:, lb:] for a in comps[f][v]]
                                for v in range(2)
                            ]
                            val.append(four_points(*hemi[0]))
                            g0, g1, g2, g3 = hemi[1]
                            slo.append(four_points(g1, g0, g3, g2))
                        c_lat = cor[h : h + 1]
                        tend = [[], [], []]
                        for k in range(4):
                            u, w, z = (val[f][k] for f in range(3))
                            du, dw, dz = (slo[f][k] for f in range(3))
                            tend[0].append(c_lat * w - u * du - dz)
                            tend[1].append(-u * dw - c_lat * u)
                            tend[2].append(-u * dz - (1.0 + z) * du)
                        folded.append([fold_points(t) for t in tend])
                    at = pl.multiple_of(c * kc + i * 16, 16)
                    for f in range(d.fields):
                        for q in range(4):
                            north, south = folded[0][f][q], folded[1][f][q]
                            t = jnp.concatenate([north + south, north - south], axis=1)
                            top = t.astype(BF16)
                            high[f * 4 + q, pl.ds(at, 16)] = top
                            low[f * 4 + q, pl.ds(at, 16)] = (t - top.astype(F32)).astype(BF16)
                            edge[f * 4 + q] = t[:8]
                    return _

                lax.fori_loop(0, kc // 16, block, None)
                return _

            lax.fori_loop(0, 3, rows, None)

            def field(f, _):
                for q in range(4):
                    p, cc = divmod(q, 2)
                    both = mul(back[p, cc], high[f * 4 + q, : d.half], ((1,), (0,)))
                    spec = both[: d.half] + both[d.half :]
                    spec = spec + mul(back[p, cc, : d.half], low[f * 4 + q, : d.half], ((1,), (0,)))
                    if p == cc:
                        sign = 1.0 - 2.0 * (lax.broadcasted_iota(jnp.int32, (d.half, 1), 0) % 2).astype(F32)
                        scale = 0.5 / math.sqrt(d.modes) * (1.0 if p == 0 else -1.0)
                        spec = spec + (sign * scale) * edge[f * 4 + q, :1]
                    send_back[s * g + f * 4 + q] = (spec * weight[...]).astype(BF16)

                @pl.when(s < last)
                def _():
                    for off in range(1, n):
                        behind(s, f, off).start()
                    behind_own(s, f).start()

                return _

            lax.fori_loop(0, d.fields, field, None)
            return _

        lax.fori_loop(0, d.el, step, None)

        def chunk(c, _):
            for off in range(1, n):
                final(c, off).start()
            final_own(c).start()
            return _

        lax.fori_loop(0, d.nc, chunk, None)

    pl.run_scoped(
        grid,
        pltpu.VMEM((g, n, d.pl, 2 * d.lb), BF16),
        pltpu.VMEM((g, 2 * d.kc, 2 * d.lb), F32),
        pltpu.VMEM((g, 3 * d.kc, 2 * d.lb), BF16),
        pltpu.VMEM((g, 3 * d.kc, 2 * d.lb), BF16),
        pltpu.VMEM((g, 8, 2 * d.lb), F32),
    )

    is_outer = lax.rem(node, 3) == 0
    is_inner = jnp.logical_not(is_outer)
    beside = jnp.where(is_outer, 1 + node // 3, (node - 1) * 3)
    other = jnp.where(is_outer, beside, 3 - node)
    far_node = jnp.where(is_outer, 0, 3 - beside)

    def analysis(leg, raw, damp, drift, recv, lhs, own, partial, bufs, rates, mix_rows, result):
        def copy(src, dst, send_s, recv_s, c, peer):
            return pltpu.make_async_remote_copy(
                src_ref=src.at[c], dst_ref=dst.at[c], send_sem=send_s.at[c], recv_sem=recv_s.at[c],
                device_id={"node": peer}, device_id_type=MESH,
            )

        def to_inner(c):
            return copy(own, outer, own_send, o_sem, c, beside)

        def to_other(c):
            return copy(own, cross, own_send, x_recv, c, other)

        def forward(c):
            return copy(outer, far, fwd_send, y_sem, c, other)

        def to_outer(c):
            return copy(partial, cross, par_send, x_recv, c, beside)

        def fetch(i, slot):
            at = pl.ds(i * SUB, SUB)
            return [
                pltpu.make_async_copy(leg_hbm.at[at], leg.at[slot], leg_sem.at[slot, 0]),
                pltpu.make_async_copy(it_hbm.at[0, :, at], raw.at[slot, 0], leg_sem.at[slot, 1]),
                pltpu.make_async_copy(state_hbm.at[:, at], raw.at[slot, 1], leg_sem.at[slot, 2]),
                pltpu.make_async_copy(rate_hbm.at[:, at], damp.at[slot], leg_sem.at[slot, 3]),
            ]

        def fetch_spectra(c, slot):
            return pltpu.make_async_copy(
                spectra.at[:, :, :, pl.ds(c * per, per)], recv.at[slot], recv_sem.at[slot]
            )

        def arrive(c):
            for off in range(1, n):
                final(c, off).wait_recv()
            final_own(c).wait()

        for copy_in in fetch(0, 0):
            copy_in.start()

        def early(i, _):
            s, f = i // d.fields, lax.rem(i, d.fields)
            for off in range(1, n):
                behind(s, f, off).wait_recv()
            behind_own(s, f).wait()
            return _

        lax.fori_loop(0, last * d.fields, early, None)
        arrive(0)
        fetch_spectra(0, 0).start()

        def chunk(c, _):
            cslot = lax.rem(c, 2)
            fetch_spectra(c, cslot).wait()
            for s in range(d.el):
                for lb in range(d.nlb):
                    for eg in range(d.eg):
                        for f in range(d.fields):
                            for p in range(2):
                                for cc in range(2):
                                    r = (cc * d.fields + f) * d.members + eg * d.el + s
                                    tile = recv[cslot, s, lb * d.eg + eg, f * 4 + p * 2 + cc].astype(F32)
                                    for par in range(2):
                                        at = ((par * d.nlb + lb) * d.rows + r) * d.mc + p * per
                                        lhs[pl.ds(at, per), :] = tile[:, par * d.lb : (par + 1) * d.lb]

            def sub(j, _):
                i = c * subs + j
                slot = lax.rem(i, 2)

                @pl.when(i + 1 < total)
                def _():
                    for copy_in in fetch(i + 1, 1 - slot):
                        copy_in.start()

                for copy_in in fetch(i, slot):
                    copy_in.wait()
                for mi in range(SUB):
                    gather_rows(
                        d,
                        drift.at[mi],
                        lambda cc, f: damp[slot, f, mi : mi + 1] * (raw[slot, 0, cc, mi, f] - raw[slot, 1, cc, mi, f]),
                    )
                for mi in range(SUB):
                    for par in range(2):
                        pieces = [
                            lhs[
                                pl.ds(
                                    (par * d.nlb + lb) * d.rows * d.mc + (mi % 2) * per + j * (SUB // 2) + mi // 2,
                                    d.rows,
                                    stride=d.mc,
                                ),
                                :,
                            ]
                            for lb in range(d.nlb)
                        ]
                        rows = jnp.concatenate(pieces, axis=1).astype(BF16)
                        cols = slice(par * half, (par + 1) * half)
                        y = mul(rows, leg[slot, mi, :, cols], ((1,), (0,)))
                        own[c, j * SUB + mi, :, cols] = (y - drift[mi, :, cols]).astype(BF16)
                return _

            lax.fori_loop(0, subs, sub, None)

            @pl.when(is_outer)
            def _():
                to_inner(c).start()

            @pl.when(is_inner)
            def _():
                to_other(c).start()

                @pl.when(c >= 1)
                def _():
                    to_inner(c - 1).wait_recv()
                    forward(c - 1).start()

            @pl.when(c + 1 < d.nc)
            def _():
                arrive(c + 1)
                fetch_spectra(c + 1, 1 - cslot).start()

            return _

        lax.fori_loop(0, d.nc, chunk, None)

        @pl.when(is_inner)
        def _():
            to_inner(d.nc - 1).wait_recv()
            forward(d.nc - 1).start()

        def load(c, slot):
            at = pl.ds(c * d.mc, d.mc)
            return [
                pltpu.make_async_copy(state_hbm.at[:, at], bufs.at[slot, 0], buf_sem.at[slot, 0]),
                pltpu.make_async_copy(it_hbm.at[0, :, at], bufs.at[slot, 1], buf_sem.at[slot, 1]),
                pltpu.make_async_copy(rate_hbm.at[:, at], rates.at[slot], buf_sem.at[slot, 2]),
            ]

        def save(c, slot):
            return pltpu.make_async_copy(result.at[slot], out.at[0, :, pl.ds(c * d.mc, d.mc)], res_sem.at[slot])

        for copy_in in load(0, 0):
            copy_in.start()
        sums[...] = jnp.zeros_like(sums)
        q_own = quad[node, node]
        q_total = quad[node, 0] + quad[node, 1] + quad[node, 2] + quad[node, 3]

        def combine(c, _):
            slot = lax.rem(c, 2)

            @pl.when(c + 1 < d.nc)
            def _():
                for copy_in in load(c + 1, 1 - slot):
                    copy_in.start()

            for copy_in in load(c, slot):
                copy_in.wait()

            @pl.when(c >= 2)
            def _():
                save(c - 2, slot).wait()

            @pl.when(is_inner)
            def _():
                to_other(c).wait_recv()
                forward(c).wait_recv()

                def mode(m, _):
                    a, b = own[c, m].astype(F32), cross[c, m].astype(F32)
                    o, y = outer[c, m].astype(F32), far[c, m].astype(F32)
                    mix = quad[beside, node] * a + quad[beside, other] * b + quad[beside, far_node] * y
                    partial[c, m] = mix.astype(BF16)
                    mix_rows[m] = (
                        q_own * a + quad[node, other] * b + quad[node, beside] * o + quad[node, far_node] * y
                    )
                    return _

                lax.fori_loop(0, d.mc, mode, None)
                to_outer(c).start()

            @pl.when(is_outer)
            def _():
                to_outer(c).wait_recv()

                def mode(m, _):
                    mix_rows[m] = q_own * own[c, m].astype(F32) + cross[c, m].astype(F32)
                    return _

                lax.fori_loop(0, d.mc, mode, None)

            def update(m, _):
                for f in range(d.fields):
                    rate = rates[slot, f, pl.ds(m, 1)]
                    scale = q_own * rate
                    below = 1.0 + scale
                    pull = q_total * rate
                    changed, start = sums[0, f], sums[1, f]
                    for cc in range(2):
                        r = (cc * d.fields + f) * d.members
                        state, spec = bufs[slot, 0, cc, m, f], bufs[slot, 1, cc, m, f]
                        mixed = mix_rows[m, r : r + d.members, :] - pull * state
                        new = (state + mixed + scale * spec) / below
                        result[slot, cc, m, f] = new
                        changed += (new - spec) * (new - spec)
                        start += state * state
                    sums[0, f] = changed
                    sums[1, f] = start
                return _

            lax.fori_loop(0, d.mc, update, None)
            save(c, slot).start()
            return _

        lax.fori_loop(0, d.nc, combine, None)
        for c in range(max(d.nc - 2, 0), d.nc):
            save(c, c % 2).wait()

        def finish(c, _):
            @pl.when(is_outer)
            def _():
                to_inner(c).wait_send()

            @pl.when(is_inner)
            def _():
                to_other(c).wait_send()
                forward(c).wait_send()
                to_outer(c).wait_send()

            for off in range(1, n):
                final(c, off).wait_send()
                for s in range(d.el):
                    ahead(s, c, off).wait_send()
            return _

        lax.fori_loop(0, d.nc, finish, None)

        def finish_early(i, _):
            for off in range(1, n):
                behind(i // d.fields, lax.rem(i, d.fields), off).wait_send()
            return _

        lax.fori_loop(0, last * d.fields, finish_early, None)

    natural = (2, d.mc, d.fields, d.members, d.degrees)
    pl.run_scoped(
        analysis,
        pltpu.VMEM((2, SUB, d.hemi, d.degrees), BF16),
        pltpu.VMEM((2, 2, 2, SUB, d.fields, d.members, d.degrees), F32),
        pltpu.VMEM((2, d.fields, SUB, d.degrees), F32),
        pltpu.VMEM((SUB, d.rows, d.degrees), F32),
        pltpu.VMEM((2, d.el, n, g, per, 2 * d.lb), BF16),
        pltpu.VMEM((2 * d.nlb * d.rows * d.mc, LANES), F32),
        pltpu.VMEM((d.nc, d.mc, d.rows, d.degrees), BF16),
        pltpu.VMEM((d.nc, d.mc, d.rows, d.degrees), BF16),
        pltpu.VMEM((2, 2) + natural, F32),
        pltpu.VMEM((2, d.fields, d.mc, d.degrees), F32),
        pltpu.VMEM((d.mc, d.rows, d.degrees), F32),
        pltpu.VMEM((2,) + natural, F32),
    )

    def spread(axis, me, count, slots, k):
        slots[me] = norms[k]
        copies = [
            pltpu.make_async_remote_copy(
                src_ref=norms.at[k], dst_ref=slots.at[me],
                send_sem=norm_sem.at[k, 0, off], recv_sem=norm_sem.at[k, 1, off],
                device_id={axis: lax.rem(me + off, count)}, device_id_type=MESH,
            )
            for off in range(1, count)
        ]
        for each in copies:
            each.start()
        for each in copies:
            each.wait()
        return sum(slots[i] for i in range(count))

    norms[...] = jnp.zeros_like(norms)
    for v in range(2):
        for f in range(d.fields):
            flat = sum(sums[v, f, :, k : k + LANES] for k in range(0, d.degrees, LANES))
            norms[0, 4 * v + f : 4 * v + f + 1, :] = jnp.sum(flat, axis=0, keepdims=True)
    norms[1] = spread("band", band, n, band_norms, 0)
    total_out[...] = spread("node", node, d.nnode, node_norms, 1)


def sweep(d, iterate, legendre, state, rate, trig, cor, weight, quadrature):
    anywhere, vmem = pl.BlockSpec(memory_space=pl.ANY), pl.BlockSpec(memory_space=pltpu.VMEM)
    line = pltpu.VMEM((d.nc, d.mc, d.rows, d.degrees), BF16)
    dma = pltpu.SemaphoreType.DMA
    back = (d.el - 1) * d.fields + d.nc
    per = d.mc // 2
    return pl.pallas_call(
        functools.partial(sweep_kernel, d),
        name="sweep",
        out_shape=(
            jax.ShapeDtypeStruct(iterate.shape, F32),
            jax.ShapeDtypeStruct((8, LANES), F32),
            jax.ShapeDtypeStruct((d.el * d.g, d.n, d.pl, 2 * d.lb), BF16),
            jax.ShapeDtypeStruct((d.el, d.n, d.g, d.pl, 2 * d.lb), BF16),
        ),
        in_specs=[anywhere] * 4 + [vmem] * 3 + [pl.BlockSpec(memory_space=pltpu.SMEM)],
        out_specs=(anywhere, vmem, anywhere, anywhere),
        scratch_shapes=[
            pltpu.VMEM((d.nc, d.el, d.n, d.g, per, 2 * d.lb), BF16),
            pltpu.VMEM((2, 2, 3, 4 * d.kc, d.half), BF16),
            pltpu.VMEM((2, 2, 2 * d.half, d.half), BF16),
            pltpu.VMEM((d.el * d.g, d.half, 2 * d.lb), BF16),
            line,
            line,
            line,
            pltpu.VMEM((2, d.fields, d.members, d.degrees), F32),
            pltpu.VMEM((2, 8, LANES), F32),
            pltpu.VMEM((d.n, 8, LANES), F32),
            pltpu.VMEM((d.nnode, 8, LANES), F32),
            dma((2, 4)),
            dma((d.el * d.nc, d.n)),
            dma((d.el * d.nc, d.n)),
            dma((d.el * d.nc,)),
            dma((1,)),
            dma((back, d.n)),
            dma((back, d.n)),
            dma((back,)),
            dma((2,)),
            dma((d.nc,)),
            dma((d.nc,)),
            dma((d.nc,)),
            dma((d.nc,)),
            dma((d.nc,)),
            dma((d.nc,)),
            dma((2, 3)),
            dma((2,)),
            dma((2, 2, d.n)),
        ],
        compiler_params=pltpu.CompilerParams(
            collective_id=1, has_side_effects=True, vmem_limit_bytes=VMEM_BYTES
        ),
    )(iterate, legendre, state, rate, trig, cor, weight, quadrature)


def fast_body(d, state0, iterate, legendre, lat_weight, coriolis, damping, quadrature):
    band = lax.axis_index("band")
    first = (band // d.eg) * d.lb
    cor = lax.dynamic_slice_in_dim(coriolis, first, d.lb, 1)
    weight = jnp.tile(lax.dynamic_slice_in_dim(lat_weight, first, d.lb, 0), 2)[None]
    iterate, state0 = jnp.swapaxes(iterate, 3, 4), jnp.swapaxes(state0, 2, 3)
    damping = jnp.swapaxes(damping, 0, 1)
    trig = jnp.asarray(trig_rows(d))
    updated, norms, _, _ = sweep(d, iterate, legendre, state0, damping, trig, cor, weight, quadrature)
    total = norms.reshape(2, 4, LANES)[:, : d.fields].sum(axis=2)
    return jnp.swapaxes(updated, 3, 4), jnp.sqrt(total[0] / (total[1] + 1e-06))


def solution(mesh):
    placed = (
        P(None, "band", None, None, None),
        P("node", None, "band", None, None, None),
        P("band", None, None),
        P(),
        P(),
        P("band", None, None),
        P(),
    )

    def call(*args):
        d = Plan(mesh.shape["band"], mesh.shape["node"], args[1].shape, args[2].shape)
        body = functools.partial(fast_body, d) if d.fits else plain_body
        return jax.shard_map(
            body,
            mesh=mesh,
            in_specs=placed,
            out_specs=(P("node", None, "band", None, None, None), P()),
            check_vma=False,
        )(*args)

    return call
```

```python
import functools
import math

import jax
import jax.numpy as jnp
import numpy as np
from jax import lax
from jax.experimental import pallas as pl
from jax.experimental.pallas import tpu as pltpu
from jax.sharding import PartitionSpec as P

MESH = pl.DeviceIdType.MESH
F32, BF16 = jnp.float32, jnp.bfloat16
VMEM_BYTES = 63_000_000
LANES = 128
SUB = 4


def split_bf16(x):
    high = lax.reduce_precision(x, 8, 7)
    return high.astype(jnp.bfloat16), (x - high).astype(jnp.bfloat16)


def dft_table(parity, nband, local_modes, modes, points):
    fine = 32
    coarse = modes // fine
    column = lax.iota(jnp.int32, modes)
    pairs = local_modes // 2
    part = column // pairs % 2
    wave = column // local_modes * local_modes + column % pairs * 2 + parity
    unit = 2.0 * math.pi / points

    def angle(index):
        return (index % points).astype(jnp.float32) * unit

    big = angle(
        lax.iota(jnp.int32, coarse)[:, None] * fine * wave[None] + part[None] * (points // 4)
    )
    small = angle(lax.iota(jnp.int32, fine)[:, None] * wave[None])
    cos_big, sin_big = jnp.cos(big)[:, None], jnp.sin(big)[:, None]
    cos_small, sin_small = jnp.cos(small)[None], jnp.sin(small)[None]
    scale = 1.0 / math.sqrt(modes)
    slope_scale = wave.astype(jnp.float32) * (scale / modes)
    value = (cos_big * cos_small - sin_big * sin_small).reshape(modes, modes) * scale
    slope = -(sin_big * cos_small + cos_big * sin_small).reshape(modes, modes) * slope_scale
    return split_bf16(value), split_bf16(slope)


def mul(a, b, dims):
    return lax.dot_general(a, b, (dims, ((), ())), preferred_element_type=jnp.float32)


def plain_body(state0, iterate, legendre, lat_weight, coriolis, damping, quadrature):
    spec = iterate[0]
    degrees = legendre.shape[2]
    half = degrees // 2
    local_modes, hemi = legendre.shape[:2]
    members, fields = spec.shape[2:4]
    nband = lax.axis_size("band")
    nnode = lax.axis_size("node")
    modes = local_modes * nband
    points = 2 * modes
    pairs = local_modes // 2
    lat_rows = hemi // nband
    node = lax.axis_index("node")
    band = lax.axis_index("band")
    tables = [dft_table(p, nband, local_modes, modes, points) for p in range(2)]
    cor = lax.dynamic_slice_in_dim(coriolis, band * lat_rows, lat_rows, 1)
    weight = lax.dynamic_slice_in_dim(lat_weight, band * lat_rows, lat_rows, 0)
    quad_row = lax.dynamic_slice_in_dim(quadrature, node, 1, 0)[0]
    diag = lax.dynamic_slice(quadrature, (node, node), (1, 1))[0, 0]
    is_even = lax.iota(jnp.int32, degrees) < half
    rate = damping[None, :, None]

    groups = 2
    ens = members // groups

    def synthesis(first):
        coeff = spec[:, :, first : first + ens].astype(jnp.bfloat16)
        coeff = coeff.transpose(1, 0, 3, 2, 4)
        zero = jnp.zeros((), jnp.bfloat16)
        rows = jnp.stack([jnp.where(is_even, coeff, zero), jnp.where(is_even, zero, coeff)], axis=1)
        rows = rows.reshape(local_modes, 4 * fields * ens, degrees)
        four = jnp.einsum("mrj,mlj->mrl", rows, legendre, preferred_element_type=jnp.float32)
        four = four.astype(jnp.bfloat16)
        four = four.reshape(pairs, 2, 2, 2, fields, ens, nband, lat_rows)
        four = four.transpose(6, 1, 3, 0, 2, 4, 5, 7)
        four = four.reshape(nband, 2, 2, pairs, 2 * fields * ens * lat_rows)
        return lax.all_to_all(four, "band", split_axis=0, concat_axis=0, tiled=True)

    def grid_step(four):
        shape = (modes, 2, fields, ens * lat_rows)
        parts = []
        for p in range(2):
            x = four[:, p].reshape(modes, -1)
            pair = []
            for high, low in tables[p]:
                dims = ((1,), (0,))
                pair.append((mul(high, x, dims) + mul(low, x, dims)).reshape(shape))
            parts.append(pair)
        tends = []
        for h in range(2):
            value, slope = (
                parts[0][v] + parts[1][v] if h == 0 else parts[0][v] - parts[1][v] for v in range(2)
            )
            hemis = []
            for s in range(2):
                val, slo = (
                    g[:, 0] + g[:, 1] if s == 0 else g[:, 0] - g[:, 1] for g in (value, slope)
                )
                c = jnp.tile(cor[s], ens)
                u, v, z = (val[:, f] for f in range(3))
                du, dv, dz = (slo[:, f] for f in range(3))
                hemis.append(
                    jnp.stack(
                        [-u * du + c * v - dz, -u * dv - c * u, -u * dz - (1.0 + z) * du], axis=1
                    )
                )
            tends.append(jnp.stack([hemis[0] + hemis[1], hemis[0] - hemis[1]], axis=1))
        scale = jnp.tile(weight, 2 * fields * ens)
        spectra = []
        for p in range(2):
            z = tends[0] + tends[1] if p == 0 else tends[0] - tends[1]
            zh, zl = split_bf16(z.reshape(modes, -1))
            high, low = tables[p][0]
            dims = ((0,), (0,))
            s = mul(high, zh, dims) + mul(high, zl, dims) + mul(low, zh, dims)
            spectra.append((s * scale).astype(jnp.bfloat16).reshape(nband, 2, pairs, -1))
        out = jnp.stack(spectra, axis=1)
        return lax.all_to_all(out, "band", split_axis=0, concat_axis=0, tiled=True)

    def analysis(out, first):
        out = out.reshape(nband, 2, 2, pairs, 2, fields, ens, lat_rows)
        out = out.transpose(3, 1, 4, 2, 5, 6, 0, 7)
        out = out.reshape(local_modes, 4 * fields * ens, hemi)
        both = jnp.einsum("mrl,mlj->mrj", out, legendre, preferred_element_type=jnp.float32)
        both = both.reshape(local_modes, 2, 2, fields, ens, degrees)
        nonlinear = jnp.where(is_even, both[:, 0], both[:, 1]).transpose(1, 0, 3, 2, 4)
        part = slice(first, first + ens)
        rest = nonlinear - rate * (spec[:, :, part] - state0[:, :, part])
        gathered = lax.all_gather(rest.astype(jnp.bfloat16), "node")
        mixed = sum(quad_row[p] * gathered[p].astype(jnp.float32) for p in range(nnode))
        return mixed

    received = [synthesis(g * ens) for g in range(groups)]
    spectra = [grid_step(r) for r in received]
    mixed = [analysis(s, g * ens) for g, s in enumerate(spectra)]
    mixed = jnp.concatenate(mixed, axis=2) - jnp.sum(quad_row) * (rate * state0)
    updated = (state0 + mixed + diag * rate * spec) / (1.0 + diag * rate)
    change = jnp.sum((updated - spec) ** 2, axis=(0, 1, 2, 4))
    base = jnp.sum(state0 * state0, axis=(0, 1, 2, 4))
    total = lax.psum(jnp.stack([change, base]), ("node", "band"))
    ratio = jnp.sqrt(total[0] / (total[1] + 1e-06))
    return (updated[None], ratio)


class Plan:
    def __init__(self, nband, nnode, iterate, legendre):
        self.n, self.nnode = nband, nnode
        self.modes, self.members, self.fields, self.degrees = iterate[2:]
        self.hemi = legendre[1]
        self.ml = self.modes // nband
        self.lb = LANES
        self.nlb = self.hemi // self.lb
        self.eg = max(nband // max(self.nlb, 1), 1)
        self.items = nnode
        self.el = self.items // self.eg
        self.k = 2 * self.fields
        self.rows = self.items * self.k
        self.pl = self.ml // 2
        self.mc = 16
        self.nc = self.ml // self.mc
        self.half = self.modes // 2
        self.kc = (self.half + 16) // 3
        self.g = 4 * self.fields
        self.fits = (
            nnode == 4
            and self.fields == 3
            and self.nlb * self.eg == nband
            and self.members == nnode
            and self.eg * self.el == self.items
            and self.hemi % self.lb == 0
            and self.ml % self.mc == 0
            and self.modes % nband == 0
            and (self.half + 16) % 48 == 0
            and self.rows % 8 == 0
            and self.degrees % 256 == 0
        )


def build_tables(d, trig, fwd, back, step):
    tall, fine = 3 * d.kc // 16, 16
    short = d.half // 16

    def turn(big, small):
        cb, sb, cs, ss = trig[0, big], trig[1, big], trig[0, small], trig[1, small]
        return cb * cs - sb * ss, -(sb * cs + cb * ss)

    for p in range(2):
        ramp = (2 * lax.broadcasted_iota(jnp.int32, (1, d.half), 1) + p).astype(F32) * (1.0 / d.modes)

        def ahead(a, _):
            cos, sin = turn(pl.ds(p * tall + a, 1), pl.ds((2 * tall + short + p * fine), fine))
            inside = lax.broadcasted_iota(jnp.int32, (fine, 1), 0) + a * fine <= d.half
            cos, sin = jnp.where(inside, cos, 0.0), jnp.where(inside, sin, 0.0)
            c = a // (d.kc // 16)
            at = (a - c * (d.kc // 16)) * 16
            for cc, pair in enumerate(((cos, ramp * sin), (sin, -ramp * cos))):
                for v, t in enumerate(pair):
                    top = t.astype(BF16)
                    fwd[p, cc, c, pl.ds(pl.multiple_of(2 * v * d.kc + at, 16), 16)] = top
                    fwd[p, cc, c, pl.ds(pl.multiple_of((2 * v + 1) * d.kc + at, 16), 16)] = (
                        t - top.astype(F32)
                    ).astype(BF16)
            return _

        lax.fori_loop(step * tall // d.nc, (step + 1) * tall // d.nc, ahead, None)
        first = jnp.where(lax.broadcasted_iota(jnp.int32, (1, d.half), 1) == 0, 0.5, 1.0)

        def behind(a, _):
            pair = turn(pl.ds(2 * tall + a, 1), pl.ds(2 * tall + short + (2 + p) * fine, fine))
            for cc, t in enumerate(pair):
                t = t * first
                top = t.astype(BF16)
                at = pl.multiple_of(a * 16, 16)
                back[p, cc, pl.ds(at, 16)] = top
                back[p, cc, pl.ds(pl.multiple_of(d.half + at, 16), 16)] = (t - top.astype(F32)).astype(BF16)
            return _

        lax.fori_loop(step * short // d.nc, (step + 1) * short // d.nc, behind, None)


def trig_rows(d):
    points = 2 * d.modes
    tall, short = 3 * d.kc // 16, d.half // 16
    wave = 2 * np.arange(d.half)
    k = np.arange(d.half)
    big = [16 * np.arange(tall)[:, None] * (wave + p)[None] for p in range(2)]
    big.append(32 * np.arange(short)[:, None] * k[None])
    small = [np.arange(16)[:, None] * (wave + p)[None] for p in range(2)]
    small += [(2 * np.arange(16) + p)[:, None] * k[None] for p in range(2)]
    angle = np.concatenate(big + small) % points * (2.0 * np.pi / points)
    scale = np.where(np.arange(len(angle)) < 2 * tall + short, d.modes**-0.5, 1.0)[:, None]
    return np.stack([np.cos(angle) * scale, np.sin(angle) * scale]).astype(np.float32)


def encode(x):
    y = x * 2.0**-9
    return (y * y * y).astype(BF16)


def decode(y):
    y = y.astype(F32)
    root = jnp.exp2(jnp.log2(jnp.maximum(jnp.abs(y), 2.0**-126)) * (1.0 / 3.0)) * 2.0**9
    return jnp.where(y == 0.0, 0.0, jnp.where(y < 0.0, -root, root))


def four_points(ce, se, co, so):
    a, b, c, e = ce + se, ce - se, co + so, co - so
    return a + c, b + e, a - c, b - e


def fold_points(t):
    s13, s24, d13, d24 = t[0] + t[2], t[1] + t[3], t[0] - t[2], t[1] - t[3]
    return s13 + s24, s13 - s24, d13 + d24, d13 - d24


def sweep_kernel(
    d, it_hbm, leg_hbm, state_hbm, rate_hbm, trig, cor, weight, quad,
    out, total_out, x_hbm, spectra,
    send, fwd, back, send_back, ready, coeff, mixed_in, own_low, sums, norms, band_norms, node_norms,
    leg_sem, c_send, c_recv, a_send, a_recv, a_own, x_sem, b_send, b_recv, b_own, recv_sem,
    m_send, m_recv, buf_sem, res_sem, norm_sem,
):
    band, node = lax.axis_index("band"), lax.axis_index("node")
    n, g, half = d.n, d.g, d.degrees // 2
    per, subs = d.mc // 2, d.mc // SUB
    total = d.nc * subs
    last = d.el - 1

    near = [("band", lax.rem(band + off, n)) for off in range(1, n)]
    near += [("node", lax.rem(node + off, d.nnode)) for off in range(1, d.nnode)]
    sem = pltpu.get_barrier_semaphore()
    for axis, peer in near:
        pl.semaphore_signal(sem, inc=1, device_id={axis: peer}, device_id_type=MESH)
    pl.semaphore_wait(sem, len(near))

    def give(c, off):
        peer = lax.rem(node + off, d.nnode)
        return pltpu.make_async_remote_copy(
            src_ref=ready.at[c, peer],
            dst_ref=coeff.at[c, node],
            send_sem=c_send.at[c, off],
            recv_sem=c_recv.at[c, off],
            device_id={"node": peer},
            device_id_type=MESH,
        )

    width = d.k * d.mc

    def hand_out(raw, rows):
        def fetch(c, slot):
            return pltpu.make_async_copy(it_hbm.at[0, :, pl.ds(c * d.mc, d.mc)], raw.at[slot], leg_sem.at[slot, 0])

        fetch(0, 0).start()

        def chunk(c, _):
            slot = lax.rem(c, 2)

            @pl.when(c + 1 < d.nc)
            def _():
                fetch(c + 1, 1 - slot).start()

            fetch(c, slot).wait()

            def mode(m, _):
                for cc in range(2):
                    for f in range(d.fields):
                        y = raw[slot, cc, m, f]
                        for t in range(d.degrees // LANES):
                            rows[t, pl.ds((cc * d.fields + f) * d.mc + m, d.members, stride=width), :] = y[
                                :, t * LANES : (t + 1) * LANES
                            ]
                return _

            lax.fori_loop(0, d.mc, mode, None)
            for t in range(d.degrees // LANES):
                cols = slice(t * LANES, (t + 1) * LANES)
                for e in range(d.members):
                    ready[c, e, :, cols] = rows[t, e * width : (e + 1) * width].astype(BF16)
                mine = rows[t, pl.ds(pl.multiple_of(node * width, width), width)]
                own_low[c, :, cols] = (mine - mine.astype(BF16).astype(F32)).astype(BF16)
            coeff[c, node] = ready[c, node]
            for off in range(1, d.nnode):
                give(c, off).start()
            return _

        lax.fori_loop(0, d.nc, chunk, None)

    pl.run_scoped(
        hand_out,
        pltpu.VMEM((2, 2, d.mc, d.fields, d.members, d.degrees), F32),
        pltpu.VMEM((d.degrees // LANES, d.members * width, LANES), F32),
    )

    def ahead(s, c, off):
        peer = lax.rem(band + off, n)
        return pltpu.make_async_remote_copy(
            src_ref=send.at[c, s, peer],
            dst_ref=x_hbm.at[pl.ds(s * g, g), band, pl.ds(c * per, per)],
            send_sem=a_send.at[s * d.nc + c, off],
            recv_sem=a_recv.at[s * d.nc + c, off],
            device_id={"band": peer},
            device_id_type=MESH,
        )

    def ahead_own(s, c):
        return pltpu.make_async_copy(
            send.at[c, s, band], x_hbm.at[pl.ds(s * g, g), band, pl.ds(c * per, per)], a_own.at[s * d.nc + c]
        )

    def start_ahead(s, c):
        for off in range(1, n):
            ahead(s, c, off).start()
        ahead_own(s, c).start()

    def synthesis(rows, leg, stage):
        def fetch(i, slot):
            return pltpu.make_async_copy(leg_hbm.at[pl.ds(i * SUB, SUB)], leg.at[slot], leg_sem.at[slot, 0])

        fetch(0, 0).start()

        def chunk(c, _):
            build_tables(d, trig, fwd, back, c)
            for off in range(1, d.nnode):
                give(c, off).wait_recv()
            for p in range(d.items):
                for t in range(d.degrees // LANES):
                    rows[t, p * width : (p + 1) * width] = coeff[c, p, :, t * LANES : (t + 1) * LANES].astype(F32)

            def sub(j, _):
                i = c * subs + j
                slot = lax.rem(i, 2)

                @pl.when(i + 1 < total)
                def _():
                    fetch(i + 1, 1 - slot).start()

                fetch(i, slot).wait()
                for mi in range(SUB):
                    pieces = [
                        rows[t, pl.ds(j * SUB + mi, d.rows, stride=d.mc), :] for t in range(d.degrees // LANES)
                    ]
                    x = jnp.concatenate(pieces, axis=1).astype(BF16)
                    table = leg[slot, mi]
                    for par in range(2):
                        cols = slice(par * half, (par + 1) * half)
                        y = mul(x[:, cols], table[:, cols], ((1,), (1,)))
                        for lb in range(d.nlb):
                            at = (lb * 2 + par) * d.rows * d.mc + (mi % 2) * per + j * (SUB // 2) + mi // 2
                            stage[pl.ds(at, d.rows, stride=d.mc), :] = y[:, lb * LANES : (lb + 1) * LANES]
                return _

            lax.fori_loop(0, subs, sub, None)
            for s in range(d.el):
                for f in range(d.fields):
                    for p in range(2):
                        for cc in range(2):
                            for lb in range(d.nlb):
                                for eg in range(d.eg):
                                    r = ((eg * d.el + s) * 2 + cc) * d.fields + f
                                    tiles = [
                                        stage[pl.ds(((lb * 2 + par) * d.rows + r) * d.mc + p * per, per), :]
                                        for par in range(2)
                                    ]
                                    send[c, s, lb * d.eg + eg, (f * 2 + p) * 2 + cc] = jnp.concatenate(
                                        tiles, axis=1
                                    ).astype(BF16)
            for s in range(d.el):
                start_ahead(s, c)
            return _

        lax.fori_loop(0, d.nc, chunk, None)

    pl.run_scoped(
        synthesis,
        pltpu.VMEM((d.degrees // LANES, d.rows * d.mc, LANES), F32),
        pltpu.VMEM((2, SUB, d.hemi, d.degrees), BF16),
        pltpu.VMEM((2 * d.nlb * d.rows * d.mc, LANES), F32),
    )

    def behind(s, f, off):
        peer = lax.rem(band + off, n)
        k = s * d.fields + f
        return pltpu.make_async_remote_copy(
            src_ref=send_back.at[pl.ds(s * g + f * 4, 4), pl.ds(peer * d.pl, d.pl)],
            dst_ref=spectra.at[s, band, pl.ds(f * 4, 4)],
            send_sem=b_send.at[k, off],
            recv_sem=b_recv.at[k, off],
            device_id={"band": peer},
            device_id_type=MESH,
        )

    def behind_own(s, f):
        return pltpu.make_async_copy(
            send_back.at[pl.ds(s * g + f * 4, 4), pl.ds(band * d.pl, d.pl)],
            spectra.at[s, band, pl.ds(f * 4, 4)],
            b_own.at[s * d.fields + f],
        )

    def final(c, off):
        peer = lax.rem(band + off, n)
        k = last * d.fields + c
        return pltpu.make_async_remote_copy(
            src_ref=send_back.at[pl.ds(last * g, g), pl.ds(peer * d.pl + c * per, per)],
            dst_ref=spectra.at[last, band, :, pl.ds(c * per, per)],
            send_sem=b_send.at[k, off],
            recv_sem=b_recv.at[k, off],
            device_id={"band": peer},
            device_id_type=MESH,
        )

    def final_own(c):
        return pltpu.make_async_copy(
            send_back.at[pl.ds(last * g, g), pl.ds(band * d.pl + c * per, per)],
            spectra.at[last, band, :, pl.ds(c * per, per)],
            b_own.at[last * d.fields + c],
        )

    def grid(x, part, high, low, edge):
        kc, lb = d.kc, d.lb

        def step(s, _):
            def arrive(c, _):
                for off in range(1, n):
                    ahead(s, c, off).wait_recv()
                ahead_own(s, c).wait()
                return _

            lax.fori_loop(0, d.nc, arrive, None)
            fetch = pltpu.make_async_copy(x_hbm.at[pl.ds(s * g, g)], x, x_sem.at[0])
            fetch.start()
            fetch.wait()

            def rows(c, _):
                def field(f, _):
                    for p in range(2):
                        for cc in range(2):
                            q = p * 2 + cc
                            y = mul(fwd[p, cc, c], x[f * 4 + q].reshape(d.half, 2 * lb), ((1,), (0,)))
                            part[f * 4 + q, :kc] = y[:kc] + y[kc : 2 * kc]
                            part[f * 4 + q, kc:] = y[2 * kc : 3 * kc] + y[3 * kc :]
                    return _

                lax.fori_loop(0, d.fields, field, None)

                def block(i, _):
                    def load(f, q, v):
                        return part[f * 4 + q, pl.ds(pl.multiple_of(v * kc + i * 16, 16), 16)]

                    folded = []
                    comps = [[[load(f, q, v) for q in range(4)] for v in range(2)] for f in range(d.fields)]
                    for h in range(2):
                        val, slo = [], []
                        for f in range(d.fields):
                            hemi = [
                                [a[:, :lb] + a[:, lb:] if h == 0 else a[:, :lb] - a[:, lb:] for a in comps[f][v]]
                                for v in range(2)
                            ]
                            val.append(four_points(*hemi[0]))
                            g0, g1, g2, g3 = hemi[1]
                            slo.append(four_points(g1, g0, g3, g2))
                        c_lat = cor[h : h + 1]
                        tend = [[], [], []]
                        for k in range(4):
                            u, w, z = (val[f][k] for f in range(3))
                            du, dw, dz = (slo[f][k] for f in range(3))
                            tend[0].append(c_lat * w - u * du - dz)
                            tend[1].append(-u * dw - c_lat * u)
                            tend[2].append(-u * dz - (1.0 + z) * du)
                        folded.append([fold_points(t) for t in tend])
                    at = pl.multiple_of(c * kc + i * 16, 16)
                    for f in range(d.fields):
                        for q in range(4):
                            north, south = folded[0][f][q], folded[1][f][q]
                            t = jnp.concatenate([north + south, north - south], axis=1)
                            top = t.astype(BF16)
                            high[f * 4 + q, pl.ds(at, 16)] = top
                            low[f * 4 + q, pl.ds(at, 16)] = (t - top.astype(F32)).astype(BF16)
                            edge[f * 4 + q] = t[:8]
                    return _

                lax.fori_loop(0, kc // 16, block, None)
                return _

            lax.fori_loop(0, 3, rows, None)

            def field(f, _):
                for q in range(4):
                    p, cc = divmod(q, 2)
                    both = mul(back[p, cc], high[f * 4 + q, : d.half], ((1,), (0,)))
                    spec = both[: d.half] + both[d.half :]
                    spec = spec + mul(back[p, cc, : d.half], low[f * 4 + q, : d.half], ((1,), (0,)))
                    if p == cc:
                        sign = 1.0 - 2.0 * (lax.broadcasted_iota(jnp.int32, (d.half, 1), 0) % 2).astype(F32)
                        scale = 0.5 / math.sqrt(d.modes) * (1.0 if p == 0 else -1.0)
                        spec = spec + (sign * scale) * edge[f * 4 + q, :1]
                    send_back[s * g + f * 4 + q] = (spec * weight[...]).astype(BF16)

                @pl.when(s < last)
                def _():
                    for off in range(1, n):
                        behind(s, f, off).start()
                    behind_own(s, f).start()

                return _

            lax.fori_loop(0, d.fields, field, None)
            return _

        lax.fori_loop(0, d.el, step, None)

        def chunk(c, _):
            for off in range(1, n):
                final(c, off).start()
            final_own(c).start()
            return _

        lax.fori_loop(0, d.nc, chunk, None)

    pl.run_scoped(
        grid,
        pltpu.VMEM((g, n, d.pl, 2 * d.lb), BF16),
        pltpu.VMEM((g, 2 * d.kc, 2 * d.lb), F32),
        pltpu.VMEM((g, 3 * d.kc, 2 * d.lb), BF16),
        pltpu.VMEM((g, 3 * d.kc, 2 * d.lb), BF16),
        pltpu.VMEM((g, 8, 2 * d.lb), F32),
    )

    def home(c, off):
        peer = lax.rem(node + off, d.nnode)
        return pltpu.make_async_remote_copy(
            src_ref=ready.at[c, peer],
            dst_ref=mixed_in.at[c, node],
            send_sem=m_send.at[c, off],
            recv_sem=m_recv.at[c, off],
            device_id={"node": peer},
            device_id_type=MESH,
        )

    def analysis(leg, state_in, damp, recv, lhs, mix, bufs, rates, mix_rows, result):
        tiles = d.degrees // LANES
        tall = 8 * d.mc

        def fetch(i, slot):
            return pltpu.make_async_copy(leg_hbm.at[pl.ds(i * SUB, SUB)], leg.at[slot], leg_sem.at[slot, 0])

        def fetch_linear(c, slot):
            at = pl.ds(c * d.mc, d.mc)
            return [
                pltpu.make_async_copy(state_hbm.at[:, at], state_in.at[slot], leg_sem.at[slot, 1]),
                pltpu.make_async_copy(rate_hbm.at[:, at], damp.at[slot], leg_sem.at[slot, 2]),
            ]

        def fetch_spectra(c, slot):
            return pltpu.make_async_copy(
                spectra.at[:, :, :, pl.ds(c * per, per)], recv.at[slot], recv_sem.at[slot]
            )

        def arrive(c):
            for off in range(1, n):
                final(c, off).wait_recv()
            final_own(c).wait()

        fetch(0, 0).start()
        for copy_in in fetch_linear(0, 0):
            copy_in.start()

        def freed(c, _):
            for off in range(1, d.nnode):
                give(c, off).wait_send()
            return _

        lax.fori_loop(0, d.nc, freed, None)

        def early(i, _):
            s, f = i // d.fields, lax.rem(i, d.fields)
            for off in range(1, n):
                behind(s, f, off).wait_recv()
            behind_own(s, f).wait()
            return _

        lax.fori_loop(0, last * d.fields, early, None)
        arrive(0)
        fetch_spectra(0, 0).start()

        def chunk(c, _):
            cslot = lax.rem(c, 2)
            fetch_spectra(c, cslot).wait()
            for s in range(d.el):
                for lb in range(d.nlb):
                    for eg in range(d.eg):
                        for f in range(d.fields):
                            for p in range(2):
                                for cc in range(2):
                                    r = ((eg * d.el + s) * 2 + cc) * d.fields + f
                                    tile = recv[cslot, s, lb * d.eg + eg, f * 4 + p * 2 + cc].astype(F32)
                                    for par in range(2):
                                        at = ((par * d.nlb + lb) * d.rows + r) * d.mc + p * per
                                        lhs[pl.ds(at, per), :] = tile[:, par * d.lb : (par + 1) * d.lb]

            def sub(j, _):
                i = c * subs + j
                slot = lax.rem(i, 2)

                @pl.when(i + 1 < total)
                def _():
                    fetch(i + 1, 1 - slot).start()

                fetch(i, slot).wait()
                for mi in range(SUB):
                    for par in range(2):
                        pieces = []
                        for lb in range(d.nlb):
                            at = (par * d.nlb + lb) * d.rows * d.mc + (mi % 2) * per + j * (SUB // 2) + mi // 2
                            pieces.append(
                                jnp.concatenate(
                                    [lhs[pl.ds(at + p * width, 8, stride=d.mc), :] for p in range(d.items)], axis=0
                                )
                            )
                        x = jnp.concatenate(pieces, axis=1).astype(BF16)
                        y = mul(x, leg[slot, mi, :, par * half : (par + 1) * half], ((1,), (0,)))
                        y = [y[8 * p : 8 * p + 8] for p in range(d.items)]
                        for q in range(d.nnode):
                            z = sum(quad[q, p] * y[p] for p in range(d.items))
                            for t in range(tiles // 2):
                                mix[par * (tiles // 2) + t, pl.ds(q * tall + j * SUB + mi, 8, stride=d.mc), :] = z[
                                    :, t * LANES : (t + 1) * LANES
                                ]
                return _

            lax.fori_loop(0, subs, sub, None)

            @pl.when(c + 1 < d.nc)
            def _():
                for copy_in in fetch_linear(c + 1, 1 - cslot):
                    copy_in.start()

            for copy_in in fetch_linear(c, cslot):
                copy_in.wait()

            def linear(k, _):
                cc = k // d.fields
                f = k - cc * d.fields
                at = pl.multiple_of(k * d.mc, d.mc)
                start = state_in[cslot, cc, :, f, pl.ds(node, 1), :].reshape(d.mc, d.degrees)
                rate = damp[cslot, f]
                low = own_low[c, pl.ds(at, d.mc)].astype(F32)
                pull = []
                for p in range(d.items):
                    spec = coeff[c, p, pl.ds(at, d.mc)].astype(F32) + jnp.where(node == p, low, 0.0)
                    pull.append(rate * (spec - start))
                for q in range(d.nnode):
                    away = sum(quad[q, p] * pull[p] for p in range(d.items) if p != q)
                    for t in range(tiles):
                        cols = slice(t * LANES, (t + 1) * LANES)
                        z = mix[t, pl.ds(pl.multiple_of(q * tall + k * d.mc, d.mc), d.mc), :]
                        ready[c, q, pl.ds(at, d.mc), cols] = encode(z - away[:, cols])
                return _

            lax.fori_loop(0, d.k, linear, None)
            mixed_in[c, node] = ready[c, node]
            for off in range(1, d.nnode):
                home(c, off).start()

            @pl.when(c + 1 < d.nc)
            def _():
                arrive(c + 1)
                fetch_spectra(c + 1, 1 - cslot).start()

            return _

        lax.fori_loop(0, d.nc, chunk, None)

        def load(c, slot):
            at = pl.ds(c * d.mc, d.mc)
            return [
                pltpu.make_async_copy(state_hbm.at[:, at], bufs.at[slot, 0], buf_sem.at[slot, 0]),
                pltpu.make_async_copy(it_hbm.at[0, :, at], bufs.at[slot, 1], buf_sem.at[slot, 1]),
                pltpu.make_async_copy(rate_hbm.at[:, at], rates.at[slot], buf_sem.at[slot, 2]),
            ]

        def save(c, slot):
            return pltpu.make_async_copy(result.at[slot], out.at[0, :, pl.ds(c * d.mc, d.mc)], res_sem.at[slot])

        for copy_in in load(0, 0):
            copy_in.start()
        sums[...] = jnp.zeros_like(sums)
        q_own = quad[node, node]
        q_total = quad[node, 0] + quad[node, 1] + quad[node, 2] + quad[node, 3]

        def combine(c, _):
            slot = lax.rem(c, 2)

            @pl.when(c + 1 < d.nc)
            def _():
                for copy_in in load(c + 1, 1 - slot):
                    copy_in.start()

            for copy_in in load(c, slot):
                copy_in.wait()

            @pl.when(c >= 2)
            def _():
                save(c - 2, slot).wait()

            for off in range(1, d.nnode):
                home(c, off).wait_recv()
            for e in range(d.members):
                for t in range(tiles):
                    mix_rows[t, e * width : (e + 1) * width] = decode(mixed_in[c, e, :, t * LANES : (t + 1) * LANES])

            def update(m, _):
                for f in range(d.fields):
                    rate = rates[slot, f, pl.ds(m, 1)]
                    scale = q_own * rate
                    below = 1.0 + scale
                    pull = (q_total - q_own) * rate
                    changed, start = sums[0, f], sums[1, f]
                    for cc in range(2):
                        state, spec = bufs[slot, 0, cc, m, f], bufs[slot, 1, cc, m, f]
                        at = (cc * d.fields + f) * d.mc + m
                        mixed = jnp.concatenate(
                            [mix_rows[t, pl.ds(at, d.members, stride=width), :] for t in range(tiles)], axis=1
                        )
                        force = mixed - pull * state - scale * spec
                        new = (state + force + scale * spec) / below
                        result[slot, cc, m, f] = new
                        changed += (new - spec) * (new - spec)
                        start += state * state
                    sums[0, f] = changed
                    sums[1, f] = start
                return _

            lax.fori_loop(0, d.mc, update, None)
            save(c, slot).start()
            return _

        lax.fori_loop(0, d.nc, combine, None)
        for c in range(max(d.nc - 2, 0), d.nc):
            save(c, c % 2).wait()

        def finish(c, _):
            for off in range(1, d.nnode):
                home(c, off).wait_send()
            for off in range(1, n):
                final(c, off).wait_send()
                for s in range(d.el):
                    ahead(s, c, off).wait_send()
            return _

        lax.fori_loop(0, d.nc, finish, None)

        def finish_early(i, _):
            for off in range(1, n):
                behind(i // d.fields, lax.rem(i, d.fields), off).wait_send()
            return _

        lax.fori_loop(0, last * d.fields, finish_early, None)

    natural = (2, d.mc, d.fields, d.members, d.degrees)
    pl.run_scoped(
        analysis,
        pltpu.VMEM((2, SUB, d.hemi, d.degrees), BF16),
        pltpu.VMEM((2,) + natural, F32),
        pltpu.VMEM((2, d.fields, d.mc, d.degrees), F32),
        pltpu.VMEM((2, d.el, n, g, per, 2 * d.lb), BF16),
        pltpu.VMEM((2 * d.nlb * d.rows * d.mc + 2 * d.mc, LANES), F32),
        pltpu.VMEM((d.degrees // LANES, d.nnode * 8 * d.mc, LANES), F32),
        pltpu.VMEM((2, 2) + natural, F32),
        pltpu.VMEM((2, d.fields, d.mc, d.degrees), F32),
        pltpu.VMEM((d.degrees // LANES, d.members * width, LANES), F32),
        pltpu.VMEM((2,) + natural, F32),
    )

    def spread(axis, me, count, slots, k):
        slots[me] = norms[k]
        copies = [
            pltpu.make_async_remote_copy(
                src_ref=norms.at[k], dst_ref=slots.at[me],
                send_sem=norm_sem.at[k, 0, off], recv_sem=norm_sem.at[k, 1, off],
                device_id={axis: lax.rem(me + off, count)}, device_id_type=MESH,
            )
            for off in range(1, count)
        ]
        for each in copies:
            each.start()
        for each in copies:
            each.wait()
        return sum(slots[i] for i in range(count))

    norms[...] = jnp.zeros_like(norms)
    for v in range(2):
        for f in range(d.fields):
            flat = sum(sums[v, f, :, k : k + LANES] for k in range(0, d.degrees, LANES))
            norms[0, 4 * v + f : 4 * v + f + 1, :] = jnp.sum(flat, axis=0, keepdims=True)
    norms[1] = spread("band", band, n, band_norms, 0)
    total_out[...] = spread("node", node, d.nnode, node_norms, 1)


def sweep(d, iterate, legendre, state, rate, trig, cor, weight, quadrature):
    anywhere, vmem = pl.BlockSpec(memory_space=pl.ANY), pl.BlockSpec(memory_space=pltpu.VMEM)
    line = pltpu.VMEM((d.nc, d.nnode, d.k * d.mc, d.degrees), BF16)
    dma = pltpu.SemaphoreType.DMA
    back = (d.el - 1) * d.fields + d.nc
    per = d.mc // 2
    return pl.pallas_call(
        functools.partial(sweep_kernel, d),
        name="sweep",
        out_shape=(
            jax.ShapeDtypeStruct(iterate.shape, F32),
            jax.ShapeDtypeStruct((8, LANES), F32),
            jax.ShapeDtypeStruct((d.el * d.g, d.n, d.pl, 2 * d.lb), BF16),
            jax.ShapeDtypeStruct((d.el, d.n, d.g, d.pl, 2 * d.lb), BF16),
        ),
        in_specs=[anywhere] * 4 + [vmem] * 3 + [pl.BlockSpec(memory_space=pltpu.SMEM)],
        out_specs=(anywhere, vmem, anywhere, anywhere),
        scratch_shapes=[
            pltpu.VMEM((d.nc, d.el, d.n, d.g, per, 2 * d.lb), BF16),
            pltpu.VMEM((2, 2, 3, 4 * d.kc, d.half), BF16),
            pltpu.VMEM((2, 2, 2 * d.half, d.half), BF16),
            pltpu.VMEM((d.el * d.g, d.half, 2 * d.lb), BF16),
            line,
            line,
            line,
            pltpu.VMEM((d.nc, d.k * d.mc, d.degrees), BF16),
            pltpu.VMEM((2, d.fields, d.members, d.degrees), F32),
            pltpu.VMEM((2, 8, LANES), F32),
            pltpu.VMEM((d.n, 8, LANES), F32),
            pltpu.VMEM((d.nnode, 8, LANES), F32),
            dma((2, 3)),
            dma((d.nc, d.nnode)),
            dma((d.nc, d.nnode)),
            dma((d.el * d.nc, d.n)),
            dma((d.el * d.nc, d.n)),
            dma((d.el * d.nc,)),
            dma((1,)),
            dma((back, d.n)),
            dma((back, d.n)),
            dma((back,)),
            dma((2,)),
            dma((d.nc, d.nnode)),
            dma((d.nc, d.nnode)),
            dma((2, 3)),
            dma((2,)),
            dma((2, 2, d.n)),
        ],
        compiler_params=pltpu.CompilerParams(
            collective_id=1, has_side_effects=True, vmem_limit_bytes=VMEM_BYTES
        ),
    )(iterate, legendre, state, rate, trig, cor, weight, quadrature)


def fast_body(d, state0, iterate, legendre, lat_weight, coriolis, damping, quadrature):
    band = lax.axis_index("band")
    first = (band // d.eg) * d.lb
    cor = lax.dynamic_slice_in_dim(coriolis, first, d.lb, 1)
    weight = jnp.tile(lax.dynamic_slice_in_dim(lat_weight, first, d.lb, 0), 2)[None]
    iterate, state0 = jnp.swapaxes(iterate, 3, 4), jnp.swapaxes(state0, 2, 3)
    damping = jnp.swapaxes(damping, 0, 1)
    trig = jnp.asarray(trig_rows(d))
    updated, norms, _, _ = sweep(d, iterate, legendre, state0, damping, trig, cor, weight, quadrature)
    total = norms.reshape(2, 4, LANES)[:, : d.fields].sum(axis=2)
    return jnp.swapaxes(updated, 3, 4), jnp.sqrt(total[0] / (total[1] + 1e-06))


def solution(mesh):
    placed = (
        P(None, "band", None, None, None),
        P("node", None, "band", None, None, None),
        P("band", None, None),
        P(),
        P(),
        P("band", None, None),
        P(),
    )

    def call(*args):
        d = Plan(mesh.shape["band"], mesh.shape["node"], args[1].shape, args[2].shape)
        body = functools.partial(fast_body, d) if d.fits else plain_body
        return jax.shard_map(
            body,
            mesh=mesh,
            in_specs=placed,
            out_specs=(P("node", None, "band", None, None, None), P()),
            check_vma=False,
        )(*args)

    return call
```

```python
import functools
import math

import jax
import jax.numpy as jnp
import numpy as np
from jax import lax
from jax.experimental import pallas as pl
from jax.experimental.pallas import tpu as pltpu
from jax.sharding import PartitionSpec as P

MESH = pl.DeviceIdType.MESH
F32, BF16 = jnp.float32, jnp.bfloat16
VMEM_BYTES = 63_000_000
LANES = 128
SUB = 8


def split_bf16(x):
    high = lax.reduce_precision(x, 8, 7)
    return high.astype(jnp.bfloat16), (x - high).astype(jnp.bfloat16)


def dft_table(parity, nband, local_modes, modes, points):
    fine = 32
    coarse = modes // fine
    column = lax.iota(jnp.int32, modes)
    pairs = local_modes // 2
    part = column // pairs % 2
    wave = column // local_modes * local_modes + column % pairs * 2 + parity
    unit = 2.0 * math.pi / points

    def angle(index):
        return (index % points).astype(jnp.float32) * unit

    big = angle(
        lax.iota(jnp.int32, coarse)[:, None] * fine * wave[None] + part[None] * (points // 4)
    )
    small = angle(lax.iota(jnp.int32, fine)[:, None] * wave[None])
    cos_big, sin_big = jnp.cos(big)[:, None], jnp.sin(big)[:, None]
    cos_small, sin_small = jnp.cos(small)[None], jnp.sin(small)[None]
    scale = 1.0 / math.sqrt(modes)
    slope_scale = wave.astype(jnp.float32) * (scale / modes)
    value = (cos_big * cos_small - sin_big * sin_small).reshape(modes, modes) * scale
    slope = -(sin_big * cos_small + cos_big * sin_small).reshape(modes, modes) * slope_scale
    return split_bf16(value), split_bf16(slope)


def mul(a, b, dims):
    return lax.dot_general(a, b, (dims, ((), ())), preferred_element_type=jnp.float32)


def plain_body(state0, iterate, legendre, lat_weight, coriolis, damping, quadrature):
    spec = iterate[0]
    degrees = legendre.shape[2]
    half = degrees // 2
    local_modes, hemi = legendre.shape[:2]
    members, fields = spec.shape[2:4]
    nband = lax.axis_size("band")
    nnode = lax.axis_size("node")
    modes = local_modes * nband
    points = 2 * modes
    pairs = local_modes // 2
    lat_rows = hemi // nband
    node = lax.axis_index("node")
    band = lax.axis_index("band")
    tables = [dft_table(p, nband, local_modes, modes, points) for p in range(2)]
    cor = lax.dynamic_slice_in_dim(coriolis, band * lat_rows, lat_rows, 1)
    weight = lax.dynamic_slice_in_dim(lat_weight, band * lat_rows, lat_rows, 0)
    quad_row = lax.dynamic_slice_in_dim(quadrature, node, 1, 0)[0]
    diag = lax.dynamic_slice(quadrature, (node, node), (1, 1))[0, 0]
    is_even = lax.iota(jnp.int32, degrees) < half
    rate = damping[None, :, None]

    groups = 2
    ens = members // groups

    def synthesis(first):
        coeff = spec[:, :, first : first + ens].astype(jnp.bfloat16)
        coeff = coeff.transpose(1, 0, 3, 2, 4)
        zero = jnp.zeros((), jnp.bfloat16)
        rows = jnp.stack([jnp.where(is_even, coeff, zero), jnp.where(is_even, zero, coeff)], axis=1)
        rows = rows.reshape(local_modes, 4 * fields * ens, degrees)
        four = jnp.einsum("mrj,mlj->mrl", rows, legendre, preferred_element_type=jnp.float32)
        four = four.astype(jnp.bfloat16)
        four = four.reshape(pairs, 2, 2, 2, fields, ens, nband, lat_rows)
        four = four.transpose(6, 1, 3, 0, 2, 4, 5, 7)
        four = four.reshape(nband, 2, 2, pairs, 2 * fields * ens * lat_rows)
        return lax.all_to_all(four, "band", split_axis=0, concat_axis=0, tiled=True)

    def grid_step(four):
        shape = (modes, 2, fields, ens * lat_rows)
        parts = []
        for p in range(2):
            x = four[:, p].reshape(modes, -1)
            pair = []
            for high, low in tables[p]:
                dims = ((1,), (0,))
                pair.append((mul(high, x, dims) + mul(low, x, dims)).reshape(shape))
            parts.append(pair)
        tends = []
        for h in range(2):
            value, slope = (
                parts[0][v] + parts[1][v] if h == 0 else parts[0][v] - parts[1][v] for v in range(2)
            )
            hemis = []
            for s in range(2):
                val, slo = (
                    g[:, 0] + g[:, 1] if s == 0 else g[:, 0] - g[:, 1] for g in (value, slope)
                )
                c = jnp.tile(cor[s], ens)
                u, v, z = (val[:, f] for f in range(3))
                du, dv, dz = (slo[:, f] for f in range(3))
                hemis.append(
                    jnp.stack(
                        [-u * du + c * v - dz, -u * dv - c * u, -u * dz - (1.0 + z) * du], axis=1
                    )
                )
            tends.append(jnp.stack([hemis[0] + hemis[1], hemis[0] - hemis[1]], axis=1))
        scale = jnp.tile(weight, 2 * fields * ens)
        spectra = []
        for p in range(2):
            z = tends[0] + tends[1] if p == 0 else tends[0] - tends[1]
            zh, zl = split_bf16(z.reshape(modes, -1))
            high, low = tables[p][0]
            dims = ((0,), (0,))
            s = mul(high, zh, dims) + mul(high, zl, dims) + mul(low, zh, dims)
            spectra.append((s * scale).astype(jnp.bfloat16).reshape(nband, 2, pairs, -1))
        out = jnp.stack(spectra, axis=1)
        return lax.all_to_all(out, "band", split_axis=0, concat_axis=0, tiled=True)

    def analysis(out, first):
        out = out.reshape(nband, 2, 2, pairs, 2, fields, ens, lat_rows)
        out = out.transpose(3, 1, 4, 2, 5, 6, 0, 7)
        out = out.reshape(local_modes, 4 * fields * ens, hemi)
        both = jnp.einsum("mrl,mlj->mrj", out, legendre, preferred_element_type=jnp.float32)
        both = both.reshape(local_modes, 2, 2, fields, ens, degrees)
        nonlinear = jnp.where(is_even, both[:, 0], both[:, 1]).transpose(1, 0, 3, 2, 4)
        part = slice(first, first + ens)
        rest = nonlinear - rate * (spec[:, :, part] - state0[:, :, part])
        gathered = lax.all_gather(rest.astype(jnp.bfloat16), "node")
        mixed = sum(quad_row[p] * gathered[p].astype(jnp.float32) for p in range(nnode))
        return mixed

    received = [synthesis(g * ens) for g in range(groups)]
    spectra = [grid_step(r) for r in received]
    mixed = [analysis(s, g * ens) for g, s in enumerate(spectra)]
    mixed = jnp.concatenate(mixed, axis=2) - jnp.sum(quad_row) * (rate * state0)
    updated = (state0 + mixed + diag * rate * spec) / (1.0 + diag * rate)
    change = jnp.sum((updated - spec) ** 2, axis=(0, 1, 2, 4))
    base = jnp.sum(state0 * state0, axis=(0, 1, 2, 4))
    total = lax.psum(jnp.stack([change, base]), ("node", "band"))
    ratio = jnp.sqrt(total[0] / (total[1] + 1e-06))
    return (updated[None], ratio)


class Plan:
    def __init__(self, nband, nnode, iterate, legendre):
        self.n, self.nnode = nband, nnode
        self.modes, self.members, self.fields, self.degrees = iterate[2:]
        self.hemi = legendre[1]
        self.ml = self.modes // nband
        self.lb = LANES
        self.nlb = self.hemi // self.lb
        self.eg = max(nband // max(self.nlb, 1), 1)
        self.items = nnode
        self.el = self.items // self.eg
        self.k = 2 * self.fields
        self.rows = self.items * self.k
        self.pl = self.ml // 2
        self.mc = 16
        self.nc = self.ml // self.mc
        self.half = self.modes // 2
        self.kc = (self.half + 16) // 3
        self.g = 4 * self.fields
        self.fits = (
            nnode == 4
            and self.fields == 3
            and self.nlb * self.eg == nband
            and self.members == nnode
            and self.eg * self.el == self.items
            and self.hemi % self.lb == 0
            and self.ml % self.mc == 0
            and self.modes % nband == 0
            and (self.half + 16) % 48 == 0
            and self.rows % 8 == 0
            and self.degrees % 256 == 0
        )


def build_tables(d, trig, fwd, back, step):
    tall, fine = 3 * d.kc // 16, 16
    short = d.half // 16

    def turn(big, small):
        cb, sb, cs, ss = trig[0, big], trig[1, big], trig[0, small], trig[1, small]
        return cb * cs - sb * ss, -(sb * cs + cb * ss)

    for p in range(2):
        ramp = (2 * lax.broadcasted_iota(jnp.int32, (1, d.half), 1) + p).astype(F32) * (1.0 / d.modes)

        def ahead(a, _):
            cos, sin = turn(pl.ds(p * tall + a, 1), pl.ds((2 * tall + short + p * fine), fine))
            inside = lax.broadcasted_iota(jnp.int32, (fine, 1), 0) + a * fine <= d.half
            cos, sin = jnp.where(inside, cos, 0.0), jnp.where(inside, sin, 0.0)
            c = a // (d.kc // 16)
            at = (a - c * (d.kc // 16)) * 16
            for cc, pair in enumerate(((cos, ramp * sin), (sin, -ramp * cos))):
                for v, t in enumerate(pair):
                    top = t.astype(BF16)
                    fwd[p, cc, c, pl.ds(pl.multiple_of(2 * v * d.kc + at, 16), 16)] = top
                    fwd[p, cc, c, pl.ds(pl.multiple_of((2 * v + 1) * d.kc + at, 16), 16)] = (
                        t - top.astype(F32)
                    ).astype(BF16)
            return _

        lax.fori_loop(step * tall // d.nc, (step + 1) * tall // d.nc, ahead, None)
        first = jnp.where(lax.broadcasted_iota(jnp.int32, (1, d.half), 1) == 0, 0.5, 1.0)

        def behind(a, _):
            pair = turn(pl.ds(2 * tall + a, 1), pl.ds(2 * tall + short + (2 + p) * fine, fine))
            for cc, t in enumerate(pair):
                t = t * first
                top = t.astype(BF16)
                at = pl.multiple_of(a * 16, 16)
                back[p, cc, pl.ds(at, 16)] = top
                back[p, cc, pl.ds(pl.multiple_of(d.half + at, 16), 16)] = (t - top.astype(F32)).astype(BF16)
            return _

        lax.fori_loop(step * short // d.nc, (step + 1) * short // d.nc, behind, None)


def trig_rows(d):
    points = 2 * d.modes
    tall, short = 3 * d.kc // 16, d.half // 16
    wave = 2 * np.arange(d.half)
    k = np.arange(d.half)
    big = [16 * np.arange(tall)[:, None] * (wave + p)[None] for p in range(2)]
    big.append(32 * np.arange(short)[:, None] * k[None])
    small = [np.arange(16)[:, None] * (wave + p)[None] for p in range(2)]
    small += [(2 * np.arange(16) + p)[:, None] * k[None] for p in range(2)]
    angle = np.concatenate(big + small) % points * (2.0 * np.pi / points)
    scale = np.where(np.arange(len(angle)) < 2 * tall + short, d.modes**-0.5, 1.0)[:, None]
    return np.stack([np.cos(angle) * scale, np.sin(angle) * scale]).astype(np.float32)


def encode(x):
    y = x * 2.0**-9
    return (y * y * y).astype(BF16)


def decode(y):
    y = y.astype(F32)
    root = jnp.exp2(jnp.log2(jnp.maximum(jnp.abs(y), 2.0**-126)) * (1.0 / 3.0)) * 2.0**9
    return jnp.where(y == 0.0, 0.0, jnp.where(y < 0.0, -root, root))


def four_points(ce, se, co, so):
    a, b, c, e = ce + se, ce - se, co + so, co - so
    return a + c, b + e, a - c, b - e


def fold_points(t):
    s13, s24, d13, d24 = t[0] + t[2], t[1] + t[3], t[0] - t[2], t[1] - t[3]
    return s13 + s24, s13 - s24, d13 + d24, d13 - d24


def sweep_kernel(
    d, it_hbm, leg_hbm, state_hbm, rate_hbm, trig, cor, weight, quad,
    out, total_out, x_hbm, spectra,
    send, fwd, back, send_back, ready, coeff, mixed_in, own_low, sums, norms, band_norms, node_norms,
    leg_sem, c_send, c_recv, a_send, a_recv, a_own, x_sem, b_send, b_recv, b_own, recv_sem,
    m_send, m_recv, buf_sem, res_sem, norm_sem,
):
    band, node = lax.axis_index("band"), lax.axis_index("node")
    n, g, half = d.n, d.g, d.degrees // 2
    per, subs = d.mc // 2, d.mc // SUB
    total = d.nc * subs
    last = d.el - 1

    near = [("band", lax.rem(band + off, n)) for off in range(1, n)]
    near += [("node", lax.rem(node + off, d.nnode)) for off in range(1, d.nnode)]
    sem = pltpu.get_barrier_semaphore()
    for axis, peer in near:
        pl.semaphore_signal(sem, inc=1, device_id={axis: peer}, device_id_type=MESH)
    pl.semaphore_wait(sem, len(near))

    def give(c, off):
        peer = lax.rem(node + off, d.nnode)
        return pltpu.make_async_remote_copy(
            src_ref=ready.at[c, peer],
            dst_ref=coeff.at[c, node],
            send_sem=c_send.at[c, off],
            recv_sem=c_recv.at[c, off],
            device_id={"node": peer},
            device_id_type=MESH,
        )

    width = d.k * d.mc

    def hand_out(raw, rows):
        def fetch(c, slot):
            return pltpu.make_async_copy(it_hbm.at[0, :, pl.ds(c * d.mc, d.mc)], raw.at[slot], leg_sem.at[slot, 0])

        fetch(0, 0).start()

        def chunk(c, _):
            slot = lax.rem(c, 2)

            @pl.when(c + 1 < d.nc)
            def _():
                fetch(c + 1, 1 - slot).start()

            fetch(c, slot).wait()

            def mode(m, _):
                for cc in range(2):
                    for f in range(d.fields):
                        y = raw[slot, cc, m, f]
                        for t in range(d.degrees // LANES):
                            rows[t, pl.ds((cc * d.fields + f) * d.mc + m, d.members, stride=width), :] = y[
                                :, t * LANES : (t + 1) * LANES
                            ]
                return _

            lax.fori_loop(0, d.mc, mode, None)
            for t in range(d.degrees // LANES):
                cols = slice(t * LANES, (t + 1) * LANES)
                for e in range(d.members):
                    ready[c, e, :, cols] = rows[t, e * width : (e + 1) * width].astype(BF16)
                mine = rows[t, pl.ds(pl.multiple_of(node * width, width), width)]
                own_low[c, :, cols] = (mine - mine.astype(BF16).astype(F32)).astype(BF16)
            coeff[c, node] = ready[c, node]
            for off in range(1, d.nnode):
                give(c, off).start()
            return _

        lax.fori_loop(0, d.nc, chunk, None)

    pl.run_scoped(
        hand_out,
        pltpu.VMEM((2, 2, d.mc, d.fields, d.members, d.degrees), F32),
        pltpu.VMEM((d.degrees // LANES, d.members * width, LANES), F32),
    )

    def ahead(s, c, off):
        peer = lax.rem(band + off, n)
        return pltpu.make_async_remote_copy(
            src_ref=send.at[c, s, peer],
            dst_ref=x_hbm.at[pl.ds(s * g, g), band, pl.ds(c * per, per)],
            send_sem=a_send.at[s * d.nc + c, off],
            recv_sem=a_recv.at[s * d.nc + c, off],
            device_id={"band": peer},
            device_id_type=MESH,
        )

    def ahead_own(s, c):
        return pltpu.make_async_copy(
            send.at[c, s, band], x_hbm.at[pl.ds(s * g, g), band, pl.ds(c * per, per)], a_own.at[s * d.nc + c]
        )

    def start_ahead(s, c):
        for off in range(1, n):
            ahead(s, c, off).start()
        ahead_own(s, c).start()

    def synthesis(rows, leg, stage):
        def fetch(i, slot):
            return pltpu.make_async_copy(leg_hbm.at[pl.ds(i * SUB, SUB)], leg.at[slot], leg_sem.at[slot, 0])

        fetch(0, 0).start()

        def chunk(c, _):
            build_tables(d, trig, fwd, back, c)
            for off in range(1, d.nnode):
                give(c, off).wait_recv()
            for p in range(d.items):
                for t in range(d.degrees // LANES):
                    rows[t, p * width : (p + 1) * width] = coeff[c, p, :, t * LANES : (t + 1) * LANES].astype(F32)

            def sub(j, _):
                i = c * subs + j
                slot = lax.rem(i, 2)

                @pl.when(i + 1 < total)
                def _():
                    fetch(i + 1, 1 - slot).start()

                fetch(i, slot).wait()
                for mi in range(SUB):
                    pieces = [
                        rows[t, pl.ds(j * SUB + mi, d.rows, stride=d.mc), :] for t in range(d.degrees // LANES)
                    ]
                    x = jnp.concatenate(pieces, axis=1).astype(BF16)
                    table = leg[slot, mi]
                    for par in range(2):
                        cols = slice(par * half, (par + 1) * half)
                        y = mul(x[:, cols], table[:, cols], ((1,), (1,)))
                        for lb in range(d.nlb):
                            at = (lb * 2 + par) * d.rows * d.mc + (mi % 2) * per + j * (SUB // 2) + mi // 2
                            stage[pl.ds(at, d.rows, stride=d.mc), :] = y[:, lb * LANES : (lb + 1) * LANES]
                return _

            lax.fori_loop(0, subs, sub, None)
            for s in range(d.el):
                for f in range(d.fields):
                    for p in range(2):
                        for cc in range(2):
                            for lb in range(d.nlb):
                                for eg in range(d.eg):
                                    r = ((eg * d.el + s) * 2 + cc) * d.fields + f
                                    tiles = [
                                        stage[pl.ds(((lb * 2 + par) * d.rows + r) * d.mc + p * per, per), :]
                                        for par in range(2)
                                    ]
                                    send[c, s, lb * d.eg + eg, (f * 2 + p) * 2 + cc] = jnp.concatenate(
                                        tiles, axis=1
                                    ).astype(BF16)
            for s in range(d.el):
                start_ahead(s, c)
            return _

        lax.fori_loop(0, d.nc, chunk, None)

    pl.run_scoped(
        synthesis,
        pltpu.VMEM((d.degrees // LANES, d.rows * d.mc, LANES), F32),
        pltpu.VMEM((2, SUB, d.hemi, d.degrees), BF16),
        pltpu.VMEM((2 * d.nlb * d.rows * d.mc, LANES), F32),
    )

    def behind(s, f, off):
        peer = lax.rem(band + off, n)
        k = s * d.fields + f
        return pltpu.make_async_remote_copy(
            src_ref=send_back.at[pl.ds(s * g + f * 4, 4), pl.ds(peer * d.pl, d.pl)],
            dst_ref=spectra.at[s, band, pl.ds(f * 4, 4)],
            send_sem=b_send.at[k, off],
            recv_sem=b_recv.at[k, off],
            device_id={"band": peer},
            device_id_type=MESH,
        )

    def behind_own(s, f):
        return pltpu.make_async_copy(
            send_back.at[pl.ds(s * g + f * 4, 4), pl.ds(band * d.pl, d.pl)],
            spectra.at[s, band, pl.ds(f * 4, 4)],
            b_own.at[s * d.fields + f],
        )

    def final(c, off):
        peer = lax.rem(band + off, n)
        k = last * d.fields + c
        return pltpu.make_async_remote_copy(
            src_ref=send_back.at[pl.ds(last * g, g), pl.ds(peer * d.pl + c * per, per)],
            dst_ref=spectra.at[last, band, :, pl.ds(c * per, per)],
            send_sem=b_send.at[k, off],
            recv_sem=b_recv.at[k, off],
            device_id={"band": peer},
            device_id_type=MESH,
        )

    def final_own(c):
        return pltpu.make_async_copy(
            send_back.at[pl.ds(last * g, g), pl.ds(band * d.pl + c * per, per)],
            spectra.at[last, band, :, pl.ds(c * per, per)],
            b_own.at[last * d.fields + c],
        )

    def grid(x, part, high, low, edge):
        kc, lb = d.kc, d.lb

        def fetch(s):
            return pltpu.make_async_copy(x_hbm.at[pl.ds(s * g, g)], x, x_sem.at[0])

        def begin(s):
            def arrive(c, _):
                for off in range(1, n):
                    ahead(s, c, off).wait_recv()
                ahead_own(s, c).wait()
                return _

            lax.fori_loop(0, d.nc, arrive, None)
            fetch(s).start()

        begin(0)

        def step(s, _):
            fetch(s).wait()

            def rows(c, _):
                def field(f, _):
                    for p in range(2):
                        for cc in range(2):
                            q = p * 2 + cc
                            y = mul(fwd[p, cc, c], x[f * 4 + q].reshape(d.half, 2 * lb), ((1,), (0,)))
                            part[f * 4 + q, :kc] = y[:kc] + y[kc : 2 * kc]
                            part[f * 4 + q, kc:] = y[2 * kc : 3 * kc] + y[3 * kc :]
                    return _

                lax.fori_loop(0, d.fields, field, None)

                def block(i, _):
                    def load(f, q, v):
                        return part[f * 4 + q, pl.ds(pl.multiple_of(v * kc + i * 16, 16), 16)]

                    folded = []
                    comps = [[[load(f, q, v) for q in range(4)] for v in range(2)] for f in range(d.fields)]
                    for h in range(2):
                        val, slo = [], []
                        for f in range(d.fields):
                            hemi = [
                                [a[:, :lb] + a[:, lb:] if h == 0 else a[:, :lb] - a[:, lb:] for a in comps[f][v]]
                                for v in range(2)
                            ]
                            val.append(four_points(*hemi[0]))
                            g0, g1, g2, g3 = hemi[1]
                            slo.append(four_points(g1, g0, g3, g2))
                        c_lat = cor[h : h + 1]
                        tend = [[], [], []]
                        for k in range(4):
                            u, w, z = (val[f][k] for f in range(3))
                            du, dw, dz = (slo[f][k] for f in range(3))
                            tend[0].append(c_lat * w - u * du - dz)
                            tend[1].append(-u * dw - c_lat * u)
                            tend[2].append(-u * dz - (1.0 + z) * du)
                        folded.append([fold_points(t) for t in tend])
                    at = pl.multiple_of(c * kc + i * 16, 16)
                    for f in range(d.fields):
                        for q in range(4):
                            north, south = folded[0][f][q], folded[1][f][q]
                            t = jnp.concatenate([north + south, north - south], axis=1)
                            top = t.astype(BF16)
                            high[f * 4 + q, pl.ds(at, 16)] = top
                            low[f * 4 + q, pl.ds(at, 16)] = (t - top.astype(F32)).astype(BF16)
                            edge[f * 4 + q] = t[:8]
                    return _

                lax.fori_loop(0, kc // 16, block, None)
                return _

            lax.fori_loop(0, 3, rows, None)

            @pl.when(s < last)
            def _():
                begin(s + 1)

            def field(f, _):
                for q in range(4):
                    p, cc = divmod(q, 2)
                    both = mul(back[p, cc], high[f * 4 + q, : d.half], ((1,), (0,)))
                    spec = both[: d.half] + both[d.half :]
                    spec = spec + mul(back[p, cc, : d.half], low[f * 4 + q, : d.half], ((1,), (0,)))
                    if p == cc:
                        sign = 1.0 - 2.0 * (lax.broadcasted_iota(jnp.int32, (d.half, 1), 0) % 2).astype(F32)
                        scale = 0.5 / math.sqrt(d.modes) * (1.0 if p == 0 else -1.0)
                        spec = spec + (sign * scale) * edge[f * 4 + q, :1]
                    send_back[s * g + f * 4 + q] = (spec * weight[...]).astype(BF16)

                @pl.when(s < last)
                def _():
                    for off in range(1, n):
                        behind(s, f, off).start()
                    behind_own(s, f).start()

                return _

            lax.fori_loop(0, d.fields, field, None)
            return _

        lax.fori_loop(0, d.el, step, None)

        def chunk(c, _):
            for off in range(1, n):
                final(c, off).start()
            final_own(c).start()
            return _

        lax.fori_loop(0, d.nc, chunk, None)

    pl.run_scoped(
        grid,
        pltpu.VMEM((g, n, d.pl, 2 * d.lb), BF16),
        pltpu.VMEM((g, 2 * d.kc, 2 * d.lb), F32),
        pltpu.VMEM((g, 3 * d.kc, 2 * d.lb), BF16),
        pltpu.VMEM((g, 3 * d.kc, 2 * d.lb), BF16),
        pltpu.VMEM((g, 8, 2 * d.lb), F32),
    )

    def home(c, off):
        peer = lax.rem(node + off, d.nnode)
        return pltpu.make_async_remote_copy(
            src_ref=ready.at[c, peer],
            dst_ref=mixed_in.at[c, node],
            send_sem=m_send.at[c, off],
            recv_sem=m_recv.at[c, off],
            device_id={"node": peer},
            device_id_type=MESH,
        )

    def analysis(leg, state_in, damp, recv, lhs, mix, bufs, rates, mix_rows, result):
        tiles = d.degrees // LANES
        tall = 8 * d.mc

        def fetch(i, slot):
            return pltpu.make_async_copy(leg_hbm.at[pl.ds(i * SUB, SUB)], leg.at[slot], leg_sem.at[slot, 0])

        def fetch_linear(c, slot):
            at = pl.ds(c * d.mc, d.mc)
            return [
                pltpu.make_async_copy(state_hbm.at[:, at], state_in.at[slot], leg_sem.at[slot, 1]),
                pltpu.make_async_copy(rate_hbm.at[:, at], damp.at[slot], leg_sem.at[slot, 2]),
            ]

        def fetch_spectra(c, slot):
            return pltpu.make_async_copy(
                spectra.at[:, :, :, pl.ds(c * per, per)], recv.at[slot], recv_sem.at[slot]
            )

        def arrive(c):
            for off in range(1, n):
                final(c, off).wait_recv()
            final_own(c).wait()

        fetch(0, 0).start()
        for copy_in in fetch_linear(0, 0):
            copy_in.start()

        def freed(c, _):
            for off in range(1, d.nnode):
                give(c, off).wait_send()
            return _

        lax.fori_loop(0, d.nc, freed, None)

        def early(i, _):
            s, f = i // d.fields, lax.rem(i, d.fields)
            for off in range(1, n):
                behind(s, f, off).wait_recv()
            behind_own(s, f).wait()
            return _

        lax.fori_loop(0, last * d.fields, early, None)
        arrive(0)
        fetch_spectra(0, 0).start()

        def chunk(c, _):
            cslot = lax.rem(c, 2)
            fetch_spectra(c, cslot).wait()
            for s in range(d.el):
                for lb in range(d.nlb):
                    for eg in range(d.eg):
                        for f in range(d.fields):
                            for p in range(2):
                                for cc in range(2):
                                    r = ((eg * d.el + s) * 2 + cc) * d.fields + f
                                    tile = recv[cslot, s, lb * d.eg + eg, f * 4 + p * 2 + cc].astype(F32)
                                    for par in range(2):
                                        at = ((par * d.nlb + lb) * d.rows + r) * d.mc + p * per
                                        lhs[pl.ds(at, per), :] = tile[:, par * d.lb : (par + 1) * d.lb]

            def sub(j, _):
                i = c * subs + j
                slot = lax.rem(i, 2)

                @pl.when(i + 1 < total)
                def _():
                    fetch(i + 1, 1 - slot).start()

                fetch(i, slot).wait()
                for mi in range(SUB):
                    for par in range(2):
                        pieces = []
                        for lb in range(d.nlb):
                            at = (par * d.nlb + lb) * d.rows * d.mc + (mi % 2) * per + j * (SUB // 2) + mi // 2
                            pieces.append(
                                jnp.concatenate(
                                    [lhs[pl.ds(at + p * width, 8, stride=d.mc), :] for p in range(d.items)], axis=0
                                )
                            )
                        x = jnp.concatenate(pieces, axis=1).astype(BF16)
                        y = mul(x, leg[slot, mi, :, par * half : (par + 1) * half], ((1,), (0,)))
                        y = [y[8 * p : 8 * p + 8] for p in range(d.items)]
                        for q in range(d.nnode):
                            z = sum(quad[q, p] * y[p] for p in range(d.items))
                            for t in range(tiles // 2):
                                mix[par * (tiles // 2) + t, pl.ds(q * tall + j * SUB + mi, 8, stride=d.mc), :] = z[
                                    :, t * LANES : (t + 1) * LANES
                                ]
                return _

            lax.fori_loop(0, subs, sub, None)

            @pl.when(c + 1 < d.nc)
            def _():
                for copy_in in fetch_linear(c + 1, 1 - cslot):
                    copy_in.start()

            for copy_in in fetch_linear(c, cslot):
                copy_in.wait()

            def linear(k, _):
                cc = k // d.fields
                f = k - cc * d.fields
                at = pl.multiple_of(k * d.mc, d.mc)
                start = state_in[cslot, cc, :, f, pl.ds(node, 1), :].reshape(d.mc, d.degrees)
                rate = damp[cslot, f]
                low = own_low[c, pl.ds(at, d.mc)].astype(F32)
                pull = []
                for p in range(d.items):
                    spec = coeff[c, p, pl.ds(at, d.mc)].astype(F32) + jnp.where(node == p, low, 0.0)
                    pull.append(rate * (spec - start))
                for q in range(d.nnode):
                    away = sum(quad[q, p] * pull[p] for p in range(d.items) if p != q)
                    for t in range(tiles):
                        cols = slice(t * LANES, (t + 1) * LANES)
                        z = mix[t, pl.ds(pl.multiple_of(q * tall + k * d.mc, d.mc), d.mc), :]
                        ready[c, q, pl.ds(at, d.mc), cols] = encode(z - away[:, cols])
                return _

            lax.fori_loop(0, d.k, linear, None)
            mixed_in[c, node] = ready[c, node]
            for off in range(1, d.nnode):
                home(c, off).start()

            @pl.when(c + 1 < d.nc)
            def _():
                arrive(c + 1)
                fetch_spectra(c + 1, 1 - cslot).start()

            return _

        lax.fori_loop(0, d.nc, chunk, None)

        def load(c, slot):
            at = pl.ds(c * d.mc, d.mc)
            return [
                pltpu.make_async_copy(state_hbm.at[:, at], bufs.at[slot, 0], buf_sem.at[slot, 0]),
                pltpu.make_async_copy(it_hbm.at[0, :, at], bufs.at[slot, 1], buf_sem.at[slot, 1]),
                pltpu.make_async_copy(rate_hbm.at[:, at], rates.at[slot], buf_sem.at[slot, 2]),
            ]

        def save(c, slot):
            return pltpu.make_async_copy(result.at[slot], out.at[0, :, pl.ds(c * d.mc, d.mc)], res_sem.at[slot])

        for copy_in in load(0, 0):
            copy_in.start()
        sums[...] = jnp.zeros_like(sums)
        q_own = quad[node, node]
        q_total = quad[node, 0] + quad[node, 1] + quad[node, 2] + quad[node, 3]

        def combine(c, _):
            slot = lax.rem(c, 2)

            @pl.when(c + 1 < d.nc)
            def _():
                for copy_in in load(c + 1, 1 - slot):
                    copy_in.start()

            for copy_in in load(c, slot):
                copy_in.wait()

            @pl.when(c >= 2)
            def _():
                save(c - 2, slot).wait()

            for off in range(1, d.nnode):
                home(c, off).wait_recv()
            for e in range(d.members):
                for t in range(tiles):
                    mix_rows[t, e * width : (e + 1) * width] = decode(mixed_in[c, e, :, t * LANES : (t + 1) * LANES])

            def update(m, _):
                for f in range(d.fields):
                    rate = rates[slot, f, pl.ds(m, 1)]
                    scale = q_own * rate
                    below = 1.0 + scale
                    pull = (q_total - q_own) * rate
                    changed, start = sums[0, f], sums[1, f]
                    for cc in range(2):
                        state, spec = bufs[slot, 0, cc, m, f], bufs[slot, 1, cc, m, f]
                        at = (cc * d.fields + f) * d.mc + m
                        mixed = jnp.concatenate(
                            [mix_rows[t, pl.ds(at, d.members, stride=width), :] for t in range(tiles)], axis=1
                        )
                        force = mixed - pull * state - scale * spec
                        new = (state + force + scale * spec) / below
                        result[slot, cc, m, f] = new
                        changed += (new - spec) * (new - spec)
                        start += state * state
                    sums[0, f] = changed
                    sums[1, f] = start
                return _

            lax.fori_loop(0, d.mc, update, None)
            save(c, slot).start()
            return _

        lax.fori_loop(0, d.nc, combine, None)
        def spread(axis, me, count, slots, k):
            slots[me] = norms[k]
            copies = [
                pltpu.make_async_remote_copy(
                    src_ref=norms.at[k], dst_ref=slots.at[me],
                    send_sem=norm_sem.at[k, 0, off], recv_sem=norm_sem.at[k, 1, off],
                    device_id={axis: lax.rem(me + off, count)}, device_id_type=MESH,
                )
                for off in range(1, count)
            ]
            for each in copies:
                each.start()
            for each in copies:
                each.wait()
            return sum(slots[i] for i in range(count))

        norms[...] = jnp.zeros_like(norms)
        for v in range(2):
            for f in range(d.fields):
                flat = sum(sums[v, f, :, k : k + LANES] for k in range(0, d.degrees, LANES))
                norms[0, 4 * v + f : 4 * v + f + 1, :] = jnp.sum(flat, axis=0, keepdims=True)
        norms[1] = spread("band", band, n, band_norms, 0)
        total_out[...] = spread("node", node, d.nnode, node_norms, 1)

        for c in range(max(d.nc - 2, 0), d.nc):
            save(c, c % 2).wait()

        def finish(c, _):
            for off in range(1, d.nnode):
                home(c, off).wait_send()
            for off in range(1, n):
                final(c, off).wait_send()
                for s in range(d.el):
                    ahead(s, c, off).wait_send()
            return _

        lax.fori_loop(0, d.nc, finish, None)

        def finish_early(i, _):
            for off in range(1, n):
                behind(i // d.fields, lax.rem(i, d.fields), off).wait_send()
            return _

        lax.fori_loop(0, last * d.fields, finish_early, None)

    natural = (2, d.mc, d.fields, d.members, d.degrees)
    pl.run_scoped(
        analysis,
        pltpu.VMEM((2, SUB, d.hemi, d.degrees), BF16),
        pltpu.VMEM((2,) + natural, F32),
        pltpu.VMEM((2, d.fields, d.mc, d.degrees), F32),
        pltpu.VMEM((2, d.el, n, g, per, 2 * d.lb), BF16),
        pltpu.VMEM((2 * d.nlb * d.rows * d.mc + 2 * d.mc, LANES), F32),
        pltpu.VMEM((d.degrees // LANES, d.nnode * 8 * d.mc, LANES), F32),
        pltpu.VMEM((2, 2) + natural, F32),
        pltpu.VMEM((2, d.fields, d.mc, d.degrees), F32),
        pltpu.VMEM((d.degrees // LANES, d.members * width, LANES), F32),
        pltpu.VMEM((2,) + natural, F32),
    )


def sweep(d, iterate, legendre, state, rate, trig, cor, weight, quadrature):
    anywhere, vmem = pl.BlockSpec(memory_space=pl.ANY), pl.BlockSpec(memory_space=pltpu.VMEM)
    line = pltpu.VMEM((d.nc, d.nnode, d.k * d.mc, d.degrees), BF16)
    dma = pltpu.SemaphoreType.DMA
    back = (d.el - 1) * d.fields + d.nc
    per = d.mc // 2
    return pl.pallas_call(
        functools.partial(sweep_kernel, d),
        name="sweep",
        out_shape=(
            jax.ShapeDtypeStruct(iterate.shape, F32),
            jax.ShapeDtypeStruct((8, LANES), F32),
            jax.ShapeDtypeStruct((d.el * d.g, d.n, d.pl, 2 * d.lb), BF16),
            jax.ShapeDtypeStruct((d.el, d.n, d.g, d.pl, 2 * d.lb), BF16),
        ),
        in_specs=[anywhere] * 4 + [vmem] * 3 + [pl.BlockSpec(memory_space=pltpu.SMEM)],
        out_specs=(anywhere, vmem, anywhere, anywhere),
        scratch_shapes=[
            pltpu.VMEM((d.nc, d.el, d.n, d.g, per, 2 * d.lb), BF16),
            pltpu.VMEM((2, 2, 3, 4 * d.kc, d.half), BF16),
            pltpu.VMEM((2, 2, 2 * d.half, d.half), BF16),
            pltpu.VMEM((d.el * d.g, d.half, 2 * d.lb), BF16),
            line,
            line,
            line,
            pltpu.VMEM((d.nc, d.k * d.mc, d.degrees), BF16),
            pltpu.VMEM((2, d.fields, d.members, d.degrees), F32),
            pltpu.VMEM((2, 8, LANES), F32),
            pltpu.VMEM((d.n, 8, LANES), F32),
            pltpu.VMEM((d.nnode, 8, LANES), F32),
            dma((2, 3)),
            dma((d.nc, d.nnode)),
            dma((d.nc, d.nnode)),
            dma((d.el * d.nc, d.n)),
            dma((d.el * d.nc, d.n)),
            dma((d.el * d.nc,)),
            dma((1,)),
            dma((back, d.n)),
            dma((back, d.n)),
            dma((back,)),
            dma((2,)),
            dma((d.nc, d.nnode)),
            dma((d.nc, d.nnode)),
            dma((2, 3)),
            dma((2,)),
            dma((2, 2, d.n)),
        ],
        compiler_params=pltpu.CompilerParams(
            collective_id=1, has_side_effects=True, vmem_limit_bytes=VMEM_BYTES
        ),
    )(iterate, legendre, state, rate, trig, cor, weight, quadrature)


def fast_body(d, state0, iterate, legendre, lat_weight, coriolis, damping, quadrature):
    band = lax.axis_index("band")
    first = (band // d.eg) * d.lb
    cor = lax.dynamic_slice_in_dim(coriolis, first, d.lb, 1)
    weight = jnp.tile(lax.dynamic_slice_in_dim(lat_weight, first, d.lb, 0), 2)[None]
    iterate, state0 = jnp.swapaxes(iterate, 3, 4), jnp.swapaxes(state0, 2, 3)
    damping = jnp.swapaxes(damping, 0, 1)
    trig = jnp.asarray(trig_rows(d))
    updated, norms, _, _ = sweep(d, iterate, legendre, state0, damping, trig, cor, weight, quadrature)
    total = norms.reshape(2, 4, LANES)[:, : d.fields].sum(axis=2)
    return jnp.swapaxes(updated, 3, 4), jnp.sqrt(total[0] / (total[1] + 1e-06))


def solution(mesh):
    placed = (
        P(None, "band", None, None, None),
        P("node", None, "band", None, None, None),
        P("band", None, None),
        P(),
        P(),
        P("band", None, None),
        P(),
    )

    def call(*args):
        d = Plan(mesh.shape["band"], mesh.shape["node"], args[1].shape, args[2].shape)
        body = functools.partial(fast_body, d) if d.fits else plain_body
        return jax.shard_map(
            body,
            mesh=mesh,
            in_specs=placed,
            out_specs=(P("node", None, "band", None, None, None), P()),
            check_vma=False,
        )(*args)

    return call
```
